256 devices in a mesh: dom: 16 (over x, y_lo, core), space: 16 (over y_hi, z).
Axes of the slice: x: 4, y: 4 (y_hi: 2, y_lo: 2; y = y_hi * 2 + y_lo), z: 8, core: 2. Of those that a mesh axis runs over, the one named last changes fastest.
Arguments:
- ancestor: int32 [64], replicated, may hold values from 0 to 63, as said below
- state: float32 [64, 3, 256, 2048], P('dom', None, 'space'), may hold values from -6 to 6
- jitter: float32 [64, 3, 256, 2048], P('dom', None, 'space'), may hold values from -4 to 4
- depth: float32 [256, 2048], P('space'), may hold values from 0.5 to 2
- coriolis: float32 [256, 2048], P('space'), may hold values from -1 to 1
- drag: float32 [256, 2048], P('space'), may hold values from 0.1 to 1
Outputs:
- forecast: float32 [64, 3, 256, 2048], P('dom', None, 'space')
The draws below stay inside these ranges and needn't reach their ends.
Inputs may be any that keep to these rules, and one draw needn't show every extreme that they name: In-place replacement: every particle either keeps its slot (ancestor[j] = j) or is replaced by a survivor p with ancestor[p] = p and p != j; a survivor is the ancestor of at most two new particles. Among the particles k*4 to k*4 + 3, at most 2 are ancestors of a particle other than themselves, and in every draw some such block has exactly 2.
All inputs are finite; a program needn't handle non-finite values.
Results may differ from the reference program's by a relative error of at most 0.00007.
Values sent between devices are 32-bit elements; how exact they have to be, the bound alone decides.
No kernel may reach another device: no remote copies, remote signals or barrier semaphores. Data moves between devices by JAX's collectives and lax.ppermute only.
A program may use at most 128 MiB of HBM per device.

```python
import math
import jax
import jax.numpy as jnp
from jax import lax

PART_DEV = 4
CAP = 2
NX = 2048
STEPS = 4
PART = 64
NY = 256


def draw_ancestor(key, part):
    groups = PART // PART_DEV
    index = jnp.arange(PART, dtype=jnp.int32)
    group_of = index // PART_DEV
    counts = jax.random.randint(jax.random.fold_in(key, 1), (groups,), 0, CAP + 1).astype(jnp.int32)
    counts = counts.at[0].set(CAP)
    scores = jax.random.randint(jax.random.fold_in(key, 2), (PART,), 0, 1 << 20).astype(jnp.int32) * PART + index
    same_group = group_of[:, None] == group_of[None, :]
    rank = jnp.sum((same_group & (scores[None, :] < scores[:, None])).astype(jnp.int32), axis=1)
    donor = rank < counts[group_of]
    donor_int = donor.astype(jnp.int32)
    total = jnp.sum(donor_int)
    kill_score = jax.random.randint(jax.random.fold_in(key, 3), (PART,), 0, 1 << 20).astype(jnp.int32) * PART + index
    kill_score = kill_score + donor_int * (1 << 30)
    kill_pos = jnp.sum((kill_score[None, :] < kill_score[:, None]).astype(jnp.int32), axis=1)
    killed = kill_pos < total
    donor_pos = jnp.cumsum(donor_int) - 1
    match = donor[None, :] & (donor_pos[None, :] == index[:, None])
    donor_of = jnp.sum(jnp.where(match, index[None, :], 0), axis=1).astype(jnp.int32)
    chosen = donor_of[jnp.clip(kill_pos, 0, PART - 1)]
    return jnp.where(killed, chosen, index).astype(jnp.int32)


def block_scale(stream_key, extent, pieces, low, high):
    loudness, own = 1.0, jax.random.fold_in(stream_key, 6)
    for position, parts in pieces:
        steps = jnp.exp(jax.random.uniform(jax.random.fold_in(own, position), (parts,), jnp.float32, low / len(pieces), high / len(pieces)))
        loudness = loudness * jnp.repeat(steps, extent[position] // parts).reshape([-1 if axis == position else 1 for axis in range(len(extent))])
    return loudness


def bell_draw(stream_key, shape, width, limit, pieces=(), kind=jnp.bfloat16):
    values = width * jax.random.normal(stream_key, shape, jnp.float32)
    if pieces:
        values = values * block_scale(stream_key, shape, pieces, -0.22, 0.18)
    return jnp.clip(values, -limit, limit).astype(kind)


def setup_inputs(seed: int = 0) -> dict:
    key_of = jax.random.split(jax.random.key(seed), 7)
    return {
        "ancestor": draw_ancestor(jax.random.fold_in(key_of[6], 71), 0),
        "state": bell_draw(key_of[1], (PART, 3, NY, NX), 1.0, 6.0, ((0, 16), (2, 16)), jnp.float32),
        "jitter": bell_draw(key_of[2], (PART, 3, NY, NX), 0.3, 4.0, ((0, 16), (2, 16)), jnp.float32),
        "depth": jnp.clip(jnp.exp(math.log(2.0) - 1.3862944 * jax.random.uniform(key_of[3], (NY, NX), jnp.float32) ** block_scale(key_of[3], (NY, NX), ((0, 16),), -0.2, 0.2)), 0.5, 2.0),
        "coriolis": jnp.clip(jax.random.uniform(key_of[4], (NY, NX), jnp.float32, -1.0, 1.0) * block_scale(key_of[4], (NY, NX), ((0, 16),), -0.4, 0.0), -1.0, 1.0),
        "drag": jnp.clip(jnp.exp(math.log(1.0) - 2.3025851 * jax.random.uniform(key_of[5], (NY, NX), jnp.float32) ** block_scale(key_of[5], (NY, NX), ((0, 16),), -0.2, 0.2)), 0.1, 1.0),
    }


time_step = 0.3


def diff_zero(values):
    padded = jnp.pad(values, [(0, 0)] * (values.ndim - 1) + [(1, 1)])
    return 0.5 * (padded[..., 2:] - padded[..., :-2])


def diff_edge(values):
    padded = jnp.pad(values, [(0, 0)] * (values.ndim - 1) + [(1, 1)], mode="edge")
    return 0.5 * (padded[..., 2:] - padded[..., :-2])


def advance(fields, depth, coriolis, drag):
    height, across, along = fields[0], fields[1], fields[2]
    for count in range(STEPS):
        flux = depth * along
        height_new = height - time_step * (diff_zero(depth * across) + 0.5 * (jnp.roll(flux, -1, 0) - jnp.roll(flux, 1, 0)))
        across_new = (across + time_step * (coriolis * along - diff_edge(height_new))) / (1.0 + time_step * drag)
        along_new = (along + time_step * (-coriolis * across - 0.5 * (jnp.roll(height_new, -1, 0) - jnp.roll(height_new, 1, 0)))) / (1.0 + time_step * drag)
        height, across, along = height_new, across_new, along_new
    return jnp.stack([height, across, along])


def reference(ancestor, state, jitter, depth, coriolis, drag):
    def member(inputs):
        source, noise = inputs
        fields = lax.dynamic_index_in_dim(state, source, 0, keepdims=False) + noise
        return advance(fields, depth, coriolis, drag)

    return lax.map(member, (ancestor, jitter))
```

```python
import functools

import jax
import jax.numpy as jnp
from jax import lax
from jax.experimental import pallas as pl
from jax.experimental.pallas import tpu as pltpu
from jax.sharding import PartitionSpec as P

STEPS = 4
CAP = 2
DT = 0.3
LANES = 128
HALO = 8
CHUNKS = ((0, 2), (2, 4))

VM = pl.BlockSpec(memory_space=pltpu.VMEM)
SM = pl.BlockSpec(memory_space=pltpu.SMEM)
ANY = pl.BlockSpec(memory_space=pl.ANY)
PARAMS = pltpu.CompilerParams(vmem_limit_bytes=24 << 20)


def pack_kernel(members, tiles, anc, state, out, sem):
    me = lax.axis_index("dom")
    bits = jnp.int32(0)
    for j in range(anc.shape[0]):
        a = anc[j]
        hit = (a != j) & (a // members == me)
        bits = bits | jnp.where(hit, jnp.left_shift(1, a % members), 0)
    first = jnp.int32(members - 1)
    for k in reversed(range(members)):
        first = jnp.where((bits >> k) & 1 == 1, k, first)
    second = jnp.int32(members - 1)
    for k in reversed(range(members)):
        second = jnp.where(((bits >> k) & 1 == 1) & (k != first), k, second)
    copies = []
    for q, p in enumerate((first, second)):
        for i in range(tiles):
            copies.append(
                pltpu.make_async_copy(
                    state.at[p, :, :, pl.ds(i * LANES, LANES)], out.at[i, q], sem.at[q * tiles + i]
                )
            )
    for c in copies:
        c.start()
    for c in copies:
        c.wait()


def pick_kernel(members, low, high, table, got, out):
    for d in range(out.shape[0]):
        for k in range(low, high):
            at = table[d * members + k]
            out[d, k - low] = got[at]


def prep_kernel(low, high, kept, routed, state, jitter, fields, top, bottom):
    tiles = routed.shape[0]
    for k in range(high - low):
        mine = kept[low + k] == 1
        for i in range(tiles):
            cols = slice(i * LANES, (i + 1) * LANES)
            value = jnp.where(mine, state[low + k, :, :, cols], routed[i, k]) + jitter[low + k, :, :, cols]
            fields[k, :, :, cols] = value
            top[k, :, :, cols] = value[:, :HALO]
            bottom[k, :, :, cols] = value[:, HALO:]


def step_kernel(low, high, fields, above, below, coef, *rest):
    out, eta, u, v = rest[-4:]
    rows, width = eta.shape
    own = fields.shape[2]
    tiles = width // LANES
    lane = lax.broadcasted_iota(jnp.int32, (rows, LANES), 1)
    first = lane == 0
    last = lane == LANES - 1
    half = 0.5 * DT

    def cols(i):
        return slice(i * LANES, (i + 1) * LANES)

    def left(x):
        return pltpu.roll(x, 1, 1)

    def right(x):
        return pltpu.roll(x, LANES - 1, 1)

    def row_diff(x):
        return pltpu.roll(x, rows - 1, 0) - pltpu.roll(x, 1, 0)

    def particle(k, carry):
        for f, ref in enumerate((eta, u, v)):
            ref[0:HALO, :] = above[k, f]
            ref[HALO : HALO + own, :] = fields[k, f]
            ref[HALO + own :, :] = below[k, f]

        def step(n, carry):
            zero = jnp.zeros((rows, LANES), jnp.float32)

            def load(i):
                uu = u[:, cols(i)]
                vv = v[:, cols(i)]
                d = coef[0, :, cols(i)]
                du = d * uu
                return uu, vv, d * vv, left(du), right(du)

            def finish(i, held, eta_new, eta_left, eta_right):
                uu, vv = held
                c = coef[1, :, cols(i)]
                r = coef[2, :, cols(i)]
                rh = half * r
                u[:, cols(i)] = r * (uu + c * vv) - rh * (eta_right - eta_left)
                v[:, cols(i)] = r * (vv - c * uu) - rh * row_diff(eta_new)

            ahead = load(0)
            shifted_before = zero
            before = None
            for i in range(tiles):
                uu, vv, dv, du_l, du_r = ahead
                if i + 1 < tiles:
                    ahead = load(i + 1)
                    du_next = ahead[4]
                else:
                    du_next = zero
                du_right = jnp.where(last, du_next, du_r)
                du_left = jnp.where(first, shifted_before, du_l)
                shifted_before = du_l
                eta_new = eta[:, cols(i)] - ((du_right - du_left) + row_diff(dv))
                eta[:, cols(i)] = eta_new
                e_l, e_r = left(eta_new), right(eta_new)
                if before is None:
                    e_left = jnp.where(first, eta_new, e_l)
                else:
                    b_i, b_held, b_new, b_left, b_l, b_r = before
                    finish(b_i, b_held, b_new, b_left, jnp.where(last, e_r, b_r))
                    e_left = jnp.where(first, b_l, e_l)
                before = (i, (uu, vv), eta_new, e_left, e_l, e_r)
            b_i, b_held, b_new, b_left, b_l, b_r = before
            finish(b_i, b_held, b_new, b_left, jnp.where(last, b_new, b_r))
            return carry

        lax.fori_loop(0, STEPS, step, 0)
        for f, ref in enumerate((eta, u, v)):
            out[k, f] = ref[HALO : HALO + own, :]
        return carry

    lax.fori_loop(0, high - low, particle, 0)


def local(ancestor, state, jitter, depth, coriolis, drag):
    members, kinds, rows, width = state.shape
    tiles = width // LANES
    blocks = lax.axis_size("dom")
    count = lax.axis_size("space")
    down = [(i, (i + 1) % count) for i in range(count)]
    up = [((i + 1) % count, i) for i in range(count)]
    me = lax.axis_index("dom")

    packed = pl.pallas_call(
        functools.partial(pack_kernel, members, tiles),
        in_specs=[SM, ANY],
        out_specs=ANY,
        out_shape=jax.ShapeDtypeStruct((tiles, CAP, kinds, rows, LANES), jnp.float32),
        scratch_shapes=[pltpu.SemaphoreType.DMA((CAP * tiles,))],
        compiler_params=PARAMS,
        name="pack",
    )(ancestor, state)
    pieces = lax.all_to_all(packed, "dom", 0, 0, tiled=True)
    pieces = pieces.reshape(blocks * CAP, kinds, rows, LANES)

    slot = jnp.arange(ancestor.shape[0], dtype=jnp.int32)
    moved = ancestor != slot
    donor = jnp.any((ancestor[:, None] == slot[None, :]) & moved[:, None], axis=0)
    same = (slot[:, None] // members == slot[None, :] // members) & (slot[:, None] < slot[None, :])
    rank = jnp.any(same & donor[:, None], axis=0).astype(jnp.int32)
    place = slot // members * CAP + rank
    table = jnp.sum(jnp.where(ancestor[:, None] == slot[None, :], place[None, :], 0), axis=1)
    kept = lax.dynamic_slice_in_dim(jnp.where(moved, 0, 1).astype(jnp.int32), me * members, members)

    coef = jnp.stack([(0.5 * DT) * depth, DT * coriolis, 1.0 / (1.0 + DT * drag)])
    coef = jnp.concatenate(
        [
            lax.ppermute(coef[:, rows - HALO :], "space", down),
            coef,
            lax.ppermute(coef[:, :HALO], "space", up),
        ],
        axis=1,
    )

    routed = []
    for low, high in CHUNKS:
        chosen = pl.pallas_call(
            functools.partial(pick_kernel, members, low, high),
            in_specs=[SM, VM],
            out_specs=VM,
            out_shape=jax.ShapeDtypeStruct((blocks, high - low, kinds, rows, LANES), jnp.float32),
            compiler_params=PARAMS,
            name="pick",
        )(table, pieces)
        routed.append(lax.all_to_all(chosen, "dom", 0, 0, tiled=True))

    out = None
    for (low, high), arrived in zip(CHUNKS, routed):
        size = high - low
        rim = jax.ShapeDtypeStruct((size, kinds, HALO, width), jnp.float32)
        fields, top, bottom = pl.pallas_call(
            functools.partial(prep_kernel, low, high),
            in_specs=[SM, VM, VM, VM],
            out_specs=(VM, VM, VM),
            out_shape=(jax.ShapeDtypeStruct((size, kinds, rows, width), jnp.float32), rim, rim),
            compiler_params=PARAMS,
            name="prep",
        )(kept, arrived, state, jitter)
        above = lax.ppermute(bottom, "space", down)
        below = lax.ppermute(top, "space", up)
        done = pl.BlockSpec((size, kinds, rows, width), lambda i, at=low // size: (at, 0, 0, 0))
        whole = [pl.BlockSpec(memory_space=pltpu.VMEM)] * 4
        out = pl.pallas_call(
            functools.partial(step_kernel, low, high),
            grid=(1,),
            in_specs=whole + ([] if out is None else [ANY]),
            out_specs=done,
            out_shape=jax.ShapeDtypeStruct(state.shape, jnp.float32),
            scratch_shapes=[pltpu.VMEM((rows + 2 * HALO, width), jnp.float32)] * 3,
            input_output_aliases={} if out is None else {4: 0},
            compiler_params=PARAMS,
            name="steps",
        )(fields, above, below, coef, *([] if out is None else [out]))
    return out


def solution(mesh):
    placed = (
        P(),
        P("dom", None, "space", None),
        P("dom", None, "space", None),
        P("space", None),
        P("space", None),
        P("space", None),
    )
    return jax.shard_map(
        local, mesh=mesh, in_specs=placed, out_specs=P("dom", None, "space", None), check_vma=False
    )
```

```python
import functools

import jax
import jax.numpy as jnp
from jax import lax
from jax.experimental import pallas as pl
from jax.experimental.pallas import tpu as pltpu
from jax.sharding import PartitionSpec as P

STEPS = 4
CAP = 2
DT = 0.3
LANES = 128
SUB = 8
DEEP = 8
RIM = (7, 7, 8)
RIMS = sum(RIM)
FROM = (0, 7, 14)
CHUNKS = ((0, 2), (2, 4))

VM = pl.BlockSpec(memory_space=pltpu.VMEM)
SM = pl.BlockSpec(memory_space=pltpu.SMEM)
HB = pl.BlockSpec(memory_space=pltpu.HBM)
PARAMS = pltpu.CompilerParams(vmem_limit_bytes=24 << 20)


def pack_kernel(members, anc, state, out, sem):
    me = lax.axis_index("dom")
    bits = jnp.int32(0)
    for j in range(anc.shape[0]):
        a = anc[j]
        hit = (a != j) & (a // members == me)
        bits = bits | jnp.where(hit, jnp.left_shift(1, a % members), 0)
    first = jnp.int32(members - 1)
    for k in reversed(range(members)):
        first = jnp.where((bits >> k) & 1 == 1, k, first)
    second = jnp.int32(members - 1)
    for k in reversed(range(members)):
        second = jnp.where(((bits >> k) & 1 == 1) & (k != first), k, second)
    copies = []
    for q, p in enumerate((first, second)):
        for f in range(state.shape[1]):
            for t in range(state.shape[2]):
                copies.append(
                    pltpu.make_async_copy(state.at[p, f, t], out.at[:, q, f, t], sem.at[len(copies)])
                )
    for c in copies:
        c.start()
    for c in copies:
        c.wait()


def coef_kernel(depth, coriolis, drag, own, top, bottom):
    rows, tiles = own.shape[1:3]
    for r in range(rows):
        at = pl.ds(r // SUB * tiles * SUB + r % SUB, tiles, stride=SUB)
        values = ((0.5 * DT) * depth[at, :], DT * coriolis[at, :], 1.0 / (1.0 + DT * drag[at, :]))
        for n, value in enumerate(values):
            own[n, r] = value
            if r < DEEP:
                top[n, r] = value
            if r >= rows - DEEP:
                bottom[n, r - (rows - DEEP)] = value


def pick_kernel(members, low, high, table, got, out):
    for d in range(out.shape[0]):
        for k in range(low, high):
            at = table[d * members + k]
            out[d, k - low] = got[at]


def prep_kernel(members, low, high, kept, routed, state, jitter, fields, top, bottom):
    kinds, rows, tiles = fields.shape[1:4]
    slab = kinds * rows
    for k in range(low, high):
        mine = kept[k] == 1
        for f in range(kinds):
            for r in range(rows):
                far = pl.ds(k * slab + f * rows + r, tiles, stride=members * slab)
                t = (k * kinds + f) * (rows // SUB) + r // SUB
                near = pl.ds(t * tiles * SUB + r % SUB, tiles, stride=SUB)
                value = jnp.where(mine, state[near, :], routed[far, :]) + jitter[near, :]
                fields[k - low, f, r] = value
                if r < RIM[f]:
                    top[k - low, FROM[f] + r] = value
                if r >= rows - RIM[f]:
                    bottom[k - low, FROM[f] + r - (rows - RIM[f])] = value


def step_kernel(low, high, fields, above, below, coef, coef_above, coef_below, *rest):
    out, eta, u, v = rest[-4:]
    kinds, rows, tiles = fields.shape[1:4]
    lane = lax.broadcasted_iota(jnp.int32, (tiles, LANES), 1)
    tile = lax.broadcasted_iota(jnp.int32, (tiles, LANES), 0)
    lane_first, lane_last = lane == 0, lane == LANES - 1
    wall_first = lane_first & (tile == 0)
    wall_last = lane_last & (tile == tiles - 1)
    half = 0.5 * DT

    def difference(x, before, after):
        x_before = pltpu.roll(jnp.where(lane_last, pltpu.roll(x, 1, 0), x), 1, 1)
        x_after = pltpu.roll(jnp.where(lane_first, pltpu.roll(x, tiles - 1, 0), x), LANES - 1, 1)
        return jnp.where(wall_last, after, x_after) - jnp.where(wall_first, before, x_before)

    def const(n, r):
        if r < 0:
            return coef_above[n, r + DEEP]
        if r >= rows:
            return coef_below[n, r - rows]
        return coef[n, r]

    def particle(k, carry):
        def start(f, r):
            if r < 0:
                return above[k, FROM[f] + r + RIM[f]]
            if r >= rows:
                return below[k, FROM[f] + r - rows]
            return fields[k, f, r]

        held = (eta, u, v)

        def store(n, f, r, value):
            if n + 1 < STEPS:
                held[f][r + DEEP] = value
            else:
                out[k, f, pl.ds(r // SUB * tiles * SUB + r % SUB, tiles, stride=SUB), :] = value

        for n in range(STEPS):
            left = STEPS - 1 - n
            get = start if n == 0 else (lambda f, r: held[f][r + DEEP])
            low_e, high_e = -(2 * left + 1), rows + 2 * left + 1
            low_v, high_v = -2 * left, rows + 2 * left
            low_u, high_u = (-(2 * left - 1), rows + 2 * left - 1) if left else (0, rows)
            zero = jnp.zeros((tiles, LANES), jnp.float32)

            def flux(r):
                return const(0, r) * get(2, r)

            flux_b, flux_m = flux(low_e - 1), flux(low_e)
            eta_b = eta_m = None
            for r in range(low_e, high_e):
                flux_a = flux(r + 1)
                across = difference(const(0, r) * get(1, r), zero, zero)
                eta_a = get(0, r) - (across + (flux_a - flux_b))
                flux_b, flux_m = flux_m, flux_a
                if low_u <= r < high_u:
                    store(n, 0, r, eta_a)
                m = r - 1
                if low_v <= m < high_v:
                    uu, vv, c, s = get(1, m), get(2, m), const(1, m), const(2, m)
                    if low_u <= m < high_u:
                        store(n, 1, m, s * (uu + c * vv - half * difference(eta_m, eta_m, eta_m)))
                    store(n, 2, m, s * (vv - c * uu - half * (eta_a - eta_b)))
                eta_b, eta_m = eta_m, eta_a
        return carry

    lax.fori_loop(0, high - low, particle, 0)


def local(ancestor, state, jitter, depth, coriolis, drag):
    members, kinds, rows, width = state.shape
    tiles, bands = width // LANES, rows // SUB
    blocks = lax.axis_size("dom")
    count = lax.axis_size("space")
    down = [(i, (i + 1) % count) for i in range(count)]
    up = [((i + 1) % count, i) for i in range(count)]
    me = lax.axis_index("dom")
    f32 = jnp.float32

    def tiled(x):
        x = x.reshape(x.shape[:-2] + (bands, SUB, tiles, LANES))
        return jnp.swapaxes(x, -3, -2)

    state_t, jitter_t = tiled(state), tiled(jitter)

    packed = pl.pallas_call(
        functools.partial(pack_kernel, members),
        in_specs=[SM, HB],
        out_specs=HB,
        out_shape=jax.ShapeDtypeStruct((tiles, CAP, kinds, bands, SUB, LANES), f32),
        scratch_shapes=[pltpu.SemaphoreType.DMA((CAP * kinds * bands,))],
        compiler_params=PARAMS,
        name="pack",
    )(ancestor, state_t)
    pieces = lax.all_to_all(packed, "dom", 0, 0, tiled=True)
    pieces = pieces.reshape(blocks * CAP, kinds * rows, LANES)

    slot = jnp.arange(ancestor.shape[0], dtype=jnp.int32)
    moved = ancestor != slot
    donor = jnp.any((ancestor[:, None] == slot[None, :]) & moved[:, None], axis=0)
    same = (slot[:, None] // members == slot[None, :] // members) & (slot[:, None] < slot[None, :])
    rank = jnp.any(same & donor[:, None], axis=0).astype(jnp.int32)
    place = slot // members * CAP + rank
    table = jnp.sum(jnp.where(ancestor[:, None] == slot[None, :], place[None, :], 0), axis=1)
    kept = lax.dynamic_slice_in_dim(jnp.where(moved, 0, 1).astype(jnp.int32), me * members, members)

    rim = jax.ShapeDtypeStruct((3, DEEP, tiles, LANES), f32)
    coef, coef_top, coef_bottom = pl.pallas_call(
        coef_kernel,
        in_specs=[VM] * 3,
        out_specs=(VM, VM, VM),
        out_shape=(jax.ShapeDtypeStruct((3, rows, tiles, LANES), f32), rim, rim),
        compiler_params=PARAMS,
        name="coef",
    )(*(tiled(x).reshape(rows * tiles, LANES) for x in (depth, coriolis, drag)))
    coef_above = lax.ppermute(coef_bottom, "space", down)
    coef_below = lax.ppermute(coef_top, "space", up)
    pieces, coef_above, coef_below, table, kept = lax.optimization_barrier(
        (pieces, coef_above, coef_below, table, kept)
    )

    chosen = pl.pallas_call(
        functools.partial(pick_kernel, members, 0, members),
        in_specs=[SM, VM],
        out_specs=VM,
        out_shape=jax.ShapeDtypeStruct((blocks, members, kinds * rows, LANES), f32),
        compiler_params=PARAMS,
        name="pick",
    )(table, pieces)
    routed = lax.all_to_all(chosen, "dom", 0, 0, tiled=True).reshape(-1, LANES)

    out = None
    chunks = []
    for low, high in CHUNKS:
        size = high - low
        rim = jax.ShapeDtypeStruct((size, RIMS, tiles, LANES), f32)
        fields, top, bottom = pl.pallas_call(
            functools.partial(prep_kernel, members, low, high),
            in_specs=[SM, VM, VM, VM],
            out_specs=(VM, VM, VM),
            out_shape=(jax.ShapeDtypeStruct((size, kinds, rows, tiles, LANES), f32), rim, rim),
            compiler_params=PARAMS,
            name="prep",
        )(kept, routed, state_t.reshape(-1, LANES), jitter_t.reshape(-1, LANES))
        above = lax.ppermute(bottom, "space", down)
        below = lax.ppermute(top, "space", up)
        chunks.append((fields, above, below))

    for (low, high), (fields, above, below) in zip(CHUNKS, chunks):
        size = high - low
        done = pl.BlockSpec((size, kinds, rows * tiles, LANES), lambda i, at=low // size: (at, 0, 0, 0))
        out = pl.pallas_call(
            functools.partial(step_kernel, low, high),
            grid=(1,),
            in_specs=[VM] * 6 + ([] if out is None else [HB]),
            out_specs=done,
            out_shape=jax.ShapeDtypeStruct((members, kinds, rows * tiles, LANES), f32),
            scratch_shapes=[pltpu.VMEM((rows + 2 * DEEP, tiles, LANES), f32)] * 3,
            input_output_aliases={} if out is None else {6: 0},
            compiler_params=PARAMS,
            name="steps",
        )(fields, above, below, coef, coef_above, coef_below, *([] if out is None else [out]))
    out = out.reshape(members, kinds, bands, tiles, SUB, LANES)
    return jnp.swapaxes(out, -3, -2).reshape(state.shape)


def solution(mesh):
    placed = (
        P(),
        P("dom", None, "space", None),
        P("dom", None, "space", None),
        P("space", None),
        P("space", None),
        P("space", None),
    )
    return jax.shard_map(
        local, mesh=mesh, in_specs=placed, out_specs=P("dom", None, "space", None), check_vma=False
    )
```

```python
import functools

import jax
import jax.numpy as jnp
from jax import lax
from jax.experimental import pallas as pl
from jax.experimental.pallas import tpu as pltpu
from jax.sharding import PartitionSpec as P

STEPS = 4
CAP = 2
DT = 0.3
LANES = 128
SUB = 8
DEEP = 8
RIM = (7, 7, 8)
RIMS = sum(RIM)
FROM = (0, 7, 14)
COEF_RIM = (8, 6, 6)
COEF_FROM = (0, 8, 14)
COEF_RIMS = sum(COEF_RIM)
CHUNKS = ((0, 2), (2, 4))

VM = pl.BlockSpec(memory_space=pltpu.VMEM)
SM = pl.BlockSpec(memory_space=pltpu.SMEM)
HB = pl.BlockSpec(memory_space=pltpu.HBM)
PARAMS = pltpu.CompilerParams(vmem_limit_bytes=24 << 20)


def pack_kernel(members, anc, state, out):
    me = lax.axis_index("dom")
    bits = jnp.int32(0)
    for j in range(anc.shape[0]):
        a = anc[j]
        hit = (a != j) & (a // members == me)
        bits = bits | jnp.where(hit, jnp.left_shift(1, a % members), 0)
    first = jnp.int32(members - 1)
    for k in reversed(range(members)):
        first = jnp.where((bits >> k) & 1 == 1, k, first)
    second = jnp.int32(members - 1)
    for k in reversed(range(members)):
        second = jnp.where(((bits >> k) & 1 == 1) & (k != first), k, second)
    for q, p in enumerate((first, second)):
        for f in range(state.shape[1]):
            for t in range(state.shape[2]):
                out[:, q, f, t] = state[p, f, t]


def coef_kernel(depth, coriolis, drag, own, top, bottom):
    rows, tiles = own.shape[1:3]
    for r in range(rows):
        at = pl.ds(r // SUB * tiles * SUB + r % SUB, tiles, stride=SUB)
        values = ((0.5 * DT) * depth[at, :], DT * coriolis[at, :], 1.0 / (1.0 + DT * drag[at, :]))
        for n, value in enumerate(values):
            own[n, r] = value
            if r < COEF_RIM[n]:
                top[COEF_FROM[n] + r] = value
            if r >= rows - COEF_RIM[n]:
                bottom[COEF_FROM[n] + r - (rows - COEF_RIM[n])] = value


def pick_kernel(members, low, high, table, got, out):
    for d in range(out.shape[0]):
        for k in range(low, high):
            at = table[d * members + k]
            out[d, k - low] = got[at]


def prep_kernel(members, low, high, kept, routed, state, jitter, fields, top, bottom):
    kinds, rows, tiles = fields.shape[1:4]
    slab = kinds * rows
    for k in range(low, high):
        mine = kept[k] == 1
        for f in range(kinds):
            for r in range(rows):
                far = pl.ds(k * slab + f * rows + r, tiles, stride=members * slab)
                t = (k * kinds + f) * (rows // SUB) + r // SUB
                near = pl.ds(t * tiles * SUB + r % SUB, tiles, stride=SUB)
                value = jnp.where(mine, state[near, :], routed[far, :]) + jitter[near, :]
                fields[k - low, f, r] = value
                if r < RIM[f]:
                    top[k - low, FROM[f] + r] = value
                if r >= rows - RIM[f]:
                    bottom[k - low, FROM[f] + r - (rows - RIM[f])] = value


def step_kernel(size, fields, above, below, coef, coef_rims, *rest):
    out, *held = rest[-4:]
    kinds, rows, tiles = fields.shape[1:4]
    lane = lax.broadcasted_iota(jnp.int32, (tiles, LANES), 1)
    tile = lax.broadcasted_iota(jnp.int32, (tiles, LANES), 0)
    lane_first, lane_last = lane == 0, lane == LANES - 1
    wall_first = lane_first & (tile == 0)
    wall_last = lane_last & (tile == tiles - 1)
    half = 0.5 * DT

    def difference(x, edge):
        before = pltpu.roll(jnp.where(lane_last, pltpu.roll(x, 1, 0), x), 1, 1)
        after = pltpu.roll(jnp.where(lane_first, pltpu.roll(x, tiles - 1, 0), x), LANES - 1, 1)
        return jnp.where(wall_last, edge, after) - jnp.where(wall_first, edge, before)

    def const(n, r):
        if r < 0:
            return coef_rims[0, COEF_FROM[n] + r + COEF_RIM[n]]
        if r >= rows:
            return coef_rims[1, COEF_FROM[n] + r - rows]
        return coef[n, r]

    def particle(k, carry):
        def get(n, f, r):
            if n:
                return held[f][n - 1, r + DEEP]
            if r < 0:
                return above[k, FROM[f] + r + RIM[f]]
            if r >= rows:
                return below[k, FROM[f] + r - rows]
            return fields[k, f, r]

        def put(n, f, r, value):
            if n < STEPS or f == 0:
                held[f][n - 1, r + DEEP] = value
            if n == STEPS and 0 <= r < rows:
                at = pl.ds(r // SUB * tiles * SUB + r % SUB, tiles, stride=SUB)
                out[k, f, at, :] = value

        for n in range(STEPS):
            left = STEPS - 1 - n
            low_u, high_u = (1 - 2 * left, rows + 2 * left - 1) if left else (0, rows)
            for r in range(-(2 * left + 1), rows + 2 * left + 1):
                across = difference(const(0, r) * get(n, 1, r), 0.0)
                along = const(0, r + 1) * get(n, 2, r + 1) - const(0, r - 1) * get(n, 2, r - 1)
                put(n + 1, 0, r, get(n, 0, r) - (across + along))
            for r in range(-2 * left, rows + 2 * left):
                uu, vv, c, s = get(n, 1, r), get(n, 2, r), const(1, r), const(2, r)
                if low_u <= r < high_u:
                    here = get(n + 1, 0, r)
                    put(n + 1, 1, r, s * (uu + c * vv - half * difference(here, here)))
                along = get(n + 1, 0, r + 1) - get(n + 1, 0, r - 1)
                put(n + 1, 2, r, s * (vv - c * uu - half * along))
        return carry

    lax.fori_loop(0, size, particle, 0)


def local(ancestor, state, jitter, depth, coriolis, drag):
    members, kinds, rows, width = state.shape
    tiles, bands = width // LANES, rows // SUB
    blocks = lax.axis_size("dom")
    count = lax.axis_size("space")
    down = [(i, (i + 1) % count) for i in range(count)]
    up = [((i + 1) % count, i) for i in range(count)]
    me = lax.axis_index("dom")
    f32 = jnp.float32

    def tiled(x):
        x = x.reshape(x.shape[:-2] + (bands, SUB, tiles, LANES))
        return jnp.swapaxes(x, -3, -2)

    state_t, jitter_t = tiled(state), tiled(jitter)

    packed = pl.pallas_call(
        functools.partial(pack_kernel, members),
        in_specs=[SM, VM],
        out_specs=VM,
        out_shape=jax.ShapeDtypeStruct((tiles, CAP, kinds, bands, SUB, LANES), f32),
        compiler_params=PARAMS,
        name="pack",
    )(ancestor, state_t)
    slot = jnp.arange(ancestor.shape[0], dtype=jnp.int32)
    moved = ancestor != slot
    donor = jnp.any((ancestor[:, None] == slot[None, :]) & moved[:, None], axis=0)
    same = (slot[:, None] // members == slot[None, :] // members) & (slot[:, None] < slot[None, :])
    rank = jnp.any(same & donor[:, None], axis=0).astype(jnp.int32)
    place = slot // members * CAP + rank
    table = jnp.sum(jnp.where(ancestor[:, None] == slot[None, :], place[None, :], 0), axis=1)
    kept = lax.dynamic_slice_in_dim(jnp.where(moved, 0, 1).astype(jnp.int32), me * members, members)

    rim = jax.ShapeDtypeStruct((COEF_RIMS, tiles, LANES), f32)
    coef, coef_top, coef_bottom = pl.pallas_call(
        coef_kernel,
        in_specs=[VM] * 3,
        out_specs=(VM, VM, VM),
        out_shape=(jax.ShapeDtypeStruct((3, rows, tiles, LANES), f32), rim, rim),
        compiler_params=PARAMS,
        name="coef",
    )(*(tiled(x).reshape(rows * tiles, LANES) for x in (depth, coriolis, drag)))
    packed, coef_top, coef_bottom = lax.optimization_barrier((packed, coef_top, coef_bottom))
    pieces = lax.all_to_all(packed, "dom", 0, 0, tiled=True)
    pieces = pieces.reshape(blocks * CAP, kinds * rows, LANES)

    odd = me % 2
    part = COEF_RIMS // 2
    coef_above = lax.ppermute(lax.dynamic_slice_in_dim(coef_bottom, odd * part, part), "space", down)
    coef_below = lax.ppermute(lax.dynamic_slice_in_dim(coef_top, odd * part, part), "space", up)
    mine = jnp.stack([coef_above, coef_below])
    other = lax.ppermute(mine, "dom", [(i, i ^ 1) for i in range(blocks)])
    coef_rims = jnp.where(
        odd == 0, jnp.concatenate([mine, other], 1), jnp.concatenate([other, mine], 1)
    )
    pieces, coef_rims, table, kept = lax.optimization_barrier((pieces, coef_rims, table, kept))

    chosen = pl.pallas_call(
        functools.partial(pick_kernel, members, 0, members),
        in_specs=[SM, VM],
        out_specs=VM,
        out_shape=jax.ShapeDtypeStruct((blocks, members, kinds * rows, LANES), f32),
        compiler_params=PARAMS,
        name="pick",
    )(table, pieces)
    routed = lax.all_to_all(chosen, "dom", 0, 0, tiled=True).reshape(-1, LANES)

    out = None
    chunks = []
    for low, high in CHUNKS:
        size = high - low
        rim = jax.ShapeDtypeStruct((size, RIMS, tiles, LANES), f32)
        fields, top, bottom = pl.pallas_call(
            functools.partial(prep_kernel, members, low, high),
            in_specs=[SM, VM, VM, VM],
            out_specs=(VM, VM, VM),
            out_shape=(jax.ShapeDtypeStruct((size, kinds, rows, tiles, LANES), f32), rim, rim),
            compiler_params=PARAMS,
            name="prep",
        )(kept, routed, state_t.reshape(-1, LANES), jitter_t.reshape(-1, LANES))
        above = lax.ppermute(bottom, "space", down)
        below = lax.ppermute(top, "space", up)
        chunks.append((fields, above, below))

    for (low, high), (fields, above, below) in zip(CHUNKS, chunks):
        size = high - low
        done = pl.BlockSpec((size, kinds, rows * tiles, LANES), lambda i, at=low // size: (at, 0, 0, 0))
        out = pl.pallas_call(
            functools.partial(step_kernel, size),
            grid=(1,),
            in_specs=[VM] * 5 + ([] if out is None else [HB]),
            out_specs=done,
            out_shape=jax.ShapeDtypeStruct((members, kinds, rows * tiles, LANES), f32),
            scratch_shapes=[pltpu.VMEM((STEPS, rows + 2 * DEEP, tiles, LANES), f32)] * 3,
            input_output_aliases={} if out is None else {5: 0},
            compiler_params=PARAMS,
            name="steps",
        )(fields, above, below, coef, coef_rims, *([] if out is None else [out]))
    out = out.reshape(members, kinds, bands, tiles, SUB, LANES)
    return jnp.swapaxes(out, -3, -2).reshape(state.shape)


def solution(mesh):
    placed = (
        P(),
        P("dom", None, "space", None),
        P("dom", None, "space", None),
        P("space", None),
        P("space", None),
        P("space", None),
    )
    return jax.shard_map(
        local, mesh=mesh, in_specs=placed, out_specs=P("dom", None, "space", None), check_vma=False
    )
```

```python
import functools

import jax
import jax.numpy as jnp
from jax import lax
from jax.experimental import pallas as pl
from jax.experimental.pallas import tpu as pltpu
from jax.sharding import PartitionSpec as P

STEPS = 4
CAP = 2
DT = 0.3
LANES = 128
SUB = 8
DEEP = 8
RIM = (7, 7, 8)
RIMS = sum(RIM)
FROM = (0, 7, 14)
COEF_RIM = (8, 6, 6)
COEF_FROM = (0, 8, 14)
COEF_RIMS = sum(COEF_RIM)
CHUNKS = ((0, 2), (2, 4))

VM = pl.BlockSpec(memory_space=pltpu.VMEM)
SM = pl.BlockSpec(memory_space=pltpu.SMEM)
HB = pl.BlockSpec(memory_space=pltpu.HBM)
PARAMS = pltpu.CompilerParams(vmem_limit_bytes=24 << 20)


def pack_kernel(members, anc, state, out):
    me = lax.axis_index("dom")
    bits = jnp.int32(0)
    for j in range(anc.shape[0]):
        a = anc[j]
        hit = (a != j) & (a // members == me)
        bits = bits | jnp.where(hit, jnp.left_shift(1, a % members), 0)
    first = jnp.int32(members - 1)
    for k in reversed(range(members)):
        first = jnp.where((bits >> k) & 1 == 1, k, first)
    second = jnp.int32(members - 1)
    for k in reversed(range(members)):
        second = jnp.where(((bits >> k) & 1 == 1) & (k != first), k, second)
    for q, p in enumerate((first, second)):
        for f in range(state.shape[1]):
            for t in range(state.shape[2]):
                out[:, q, f, t] = state[p, f, t]


def coef_kernel(depth, coriolis, drag, own, top, bottom):
    rows, tiles = own.shape[1:3]
    for r in range(rows):
        at = pl.ds(r // SUB * tiles * SUB + r % SUB, tiles, stride=SUB)
        values = ((0.5 * DT) * depth[at, :], DT * coriolis[at, :], 1.0 / (1.0 + DT * drag[at, :]))
        for n, value in enumerate(values):
            own[n, r] = value
            if r < COEF_RIM[n]:
                top[COEF_FROM[n] + r] = value
            if r >= rows - COEF_RIM[n]:
                bottom[COEF_FROM[n] + r - (rows - COEF_RIM[n])] = value


def pick_kernel(members, low, high, table, got, out):
    for d in range(out.shape[0]):
        for k in range(low, high):
            at = table[d * members + k]
            out[d, k - low] = got[at]


def prep_kernel(members, low, high, kept, routed, state, jitter, fields, top, bottom):
    kinds, rows, tiles = fields.shape[1:4]
    slab = kinds * rows
    for k in range(low, high):
        mine = kept[k] == 1
        for f in range(kinds):
            for r in range(rows):
                far = pl.ds(k * slab + f * rows + r, tiles, stride=members * slab)
                t = (k * kinds + f) * (rows // SUB) + r // SUB
                near = pl.ds(t * tiles * SUB + r % SUB, tiles, stride=SUB)
                value = jnp.where(mine, state[near, :], routed[far, :]) + jitter[near, :]
                fields[k - low, f, r] = value
                if r < RIM[f]:
                    top[k - low, FROM[f] + r] = value
                if r >= rows - RIM[f]:
                    bottom[k - low, FROM[f] + r - (rows - RIM[f])] = value


def step_kernel(size, fields, above, below, coef, coef_rims, *rest):
    out, *held = rest[-4:]
    kinds, rows, tiles = fields.shape[1:4]
    lane = lax.broadcasted_iota(jnp.int32, (tiles, LANES), 1)
    tile = lax.broadcasted_iota(jnp.int32, (tiles, LANES), 0)
    lane_first, lane_last = lane == 0, lane == LANES - 1
    wall_first = lane_first & (tile == 0)
    wall_last = lane_last & (tile == tiles - 1)
    half = 0.5 * DT

    def difference(x, edge):
        before = pltpu.roll(jnp.where(lane_last, pltpu.roll(x, 1, 0), x), 1, 1)
        after = pltpu.roll(jnp.where(lane_first, pltpu.roll(x, tiles - 1, 0), x), LANES - 1, 1)
        return jnp.where(wall_last, edge, after) - jnp.where(wall_first, edge, before)

    def const(n, r):
        if r < 0:
            return coef_rims[0, COEF_FROM[n] + r + COEF_RIM[n]]
        if r >= rows:
            return coef_rims[1, COEF_FROM[n] + r - rows]
        return coef[n, r]

    def particle(k, carry):
        def get(n, f, r):
            if n:
                return held[f][n - 1, r + DEEP]
            if r < 0:
                return above[k, FROM[f] + r + RIM[f]]
            if r >= rows:
                return below[k, FROM[f] + r - rows]
            return fields[k, f, r]

        def put(n, f, r, value):
            if n < STEPS or f == 0:
                held[f][n - 1, r + DEEP] = value
            if n == STEPS and 0 <= r < rows:
                at = pl.ds(r // SUB * tiles * SUB + r % SUB, tiles, stride=SUB)
                out[k, f, at, :] = value

        for n in range(STEPS):
            left = STEPS - 1 - n
            low_u, high_u = (1 - 2 * left, rows + 2 * left - 1) if left else (0, rows)
            for r in range(-(2 * left + 1), rows + 2 * left + 1):
                across = difference(const(0, r) * get(n, 1, r), 0.0)
                along = const(0, r + 1) * get(n, 2, r + 1) - const(0, r - 1) * get(n, 2, r - 1)
                put(n + 1, 0, r, get(n, 0, r) - (across + along))
            for r in range(-2 * left, rows + 2 * left):
                uu, vv, c, s = get(n, 1, r), get(n, 2, r), const(1, r), const(2, r)
                if low_u <= r < high_u:
                    here = get(n + 1, 0, r)
                    put(n + 1, 1, r, s * (uu + c * vv - half * difference(here, here)))
                along = get(n + 1, 0, r + 1) - get(n + 1, 0, r - 1)
                put(n + 1, 2, r, s * (vv - c * uu - half * along))
        return carry

    lax.fori_loop(0, size, particle, 0)


def local(ancestor, state, jitter, depth, coriolis, drag):
    members, kinds, rows, width = state.shape
    tiles, bands = width // LANES, rows // SUB
    blocks = lax.axis_size("dom")
    count = lax.axis_size("space")
    down = [(i, (i + 1) % count) for i in range(count)]
    up = [((i + 1) % count, i) for i in range(count)]
    me = lax.axis_index("dom")
    f32 = jnp.float32

    def tiled(x):
        x = x.reshape(x.shape[:-2] + (bands, SUB, tiles, LANES))
        return jnp.swapaxes(x, -3, -2)

    state_t, jitter_t = tiled(state), tiled(jitter)

    packed = pl.pallas_call(
        functools.partial(pack_kernel, members),
        in_specs=[SM, VM],
        out_specs=VM,
        out_shape=jax.ShapeDtypeStruct((tiles, CAP, kinds, bands, SUB, LANES), f32),
        compiler_params=PARAMS,
        name="pack",
    )(ancestor, state_t)
    slot = jnp.arange(ancestor.shape[0], dtype=jnp.int32)
    moved = ancestor != slot
    donor = jnp.any((ancestor[:, None] == slot[None, :]) & moved[:, None], axis=0)
    same = (slot[:, None] // members == slot[None, :] // members) & (slot[:, None] < slot[None, :])
    rank = jnp.any(same & donor[:, None], axis=0).astype(jnp.int32)
    place = slot // members * CAP + rank
    table = jnp.sum(jnp.where(ancestor[:, None] == slot[None, :], place[None, :], 0), axis=1)
    kept = lax.dynamic_slice_in_dim(jnp.where(moved, 0, 1).astype(jnp.int32), me * members, members)

    rim = jax.ShapeDtypeStruct((COEF_RIMS, tiles, LANES), f32)
    coef, coef_top, coef_bottom = pl.pallas_call(
        coef_kernel,
        in_specs=[VM] * 3,
        out_specs=(VM, VM, VM),
        out_shape=(jax.ShapeDtypeStruct((3, rows, tiles, LANES), f32), rim, rim),
        compiler_params=PARAMS,
        name="coef",
    )(*(tiled(x).reshape(rows * tiles, LANES) for x in (depth, coriolis, drag)))
    packed, coef_top, coef_bottom = lax.optimization_barrier((packed, coef_top, coef_bottom))
    pieces = lax.all_to_all(packed, "dom", 0, 0, tiled=True)
    pieces = pieces.reshape(blocks * CAP, kinds * rows, LANES)

    coef_rims = jnp.stack(
        [lax.ppermute(coef_bottom, "space", down), lax.ppermute(coef_top, "space", up)]
    )
    pieces, table, kept = lax.optimization_barrier((pieces, table, kept))

    chosen = pl.pallas_call(
        functools.partial(pick_kernel, members, 0, members),
        in_specs=[SM, VM],
        out_specs=VM,
        out_shape=jax.ShapeDtypeStruct((blocks, members, kinds * rows, LANES), f32),
        compiler_params=PARAMS,
        name="pick",
    )(table, pieces)
    routed = lax.all_to_all(chosen, "dom", 0, 0, tiled=True).reshape(-1, LANES)
    routed, coef_rims = lax.optimization_barrier((routed, coef_rims))

    out = None
    chunks = []
    for low, high in CHUNKS:
        size = high - low
        rim = jax.ShapeDtypeStruct((size, RIMS, tiles, LANES), f32)
        fields, top, bottom = pl.pallas_call(
            functools.partial(prep_kernel, members, low, high),
            in_specs=[SM, VM, VM, VM],
            out_specs=(VM, VM, VM),
            out_shape=(jax.ShapeDtypeStruct((size, kinds, rows, tiles, LANES), f32), rim, rim),
            compiler_params=PARAMS,
            name="prep",
        )(kept, routed, state_t.reshape(-1, LANES), jitter_t.reshape(-1, LANES))
        above = lax.ppermute(bottom, "space", down)
        below = lax.ppermute(top, "space", up)
        chunks.append((fields, above, below))

    for (low, high), (fields, above, below) in zip(CHUNKS, chunks):
        size = high - low
        done = pl.BlockSpec((size, kinds, rows * tiles, LANES), lambda i, at=low // size: (at, 0, 0, 0))
        out = pl.pallas_call(
            functools.partial(step_kernel, size),
            grid=(1,),
            in_specs=[VM] * 5 + ([] if out is None else [HB]),
            out_specs=done,
            out_shape=jax.ShapeDtypeStruct((members, kinds, rows * tiles, LANES), f32),
            scratch_shapes=[pltpu.VMEM((STEPS, rows + 2 * DEEP, tiles, LANES), f32)] * 3,
            input_output_aliases={} if out is None else {5: 0},
            compiler_params=PARAMS,
            name="steps",
        )(fields, above, below, coef, coef_rims, *([] if out is None else [out]))
    out = out.reshape(members, kinds, bands, tiles, SUB, LANES)
    return jnp.swapaxes(out, -3, -2).reshape(state.shape)


def solution(mesh):
    placed = (
        P(),
        P("dom", None, "space", None),
        P("dom", None, "space", None),
        P("space", None),
        P("space", None),
        P("space", None),
    )
    return jax.shard_map(
        local, mesh=mesh, in_specs=placed, out_specs=P("dom", None, "space", None), check_vma=False
    )
```

```python
import functools

import jax
import jax.numpy as jnp
from jax import lax
from jax.experimental import pallas as pl
from jax.experimental.pallas import tpu as pltpu
from jax.sharding import PartitionSpec as P

STEPS = 4
CAP = 2
DT = 0.3
LANES = 128
SUB = 8
DEEP = 8
RIM = (7, 7, 8)
RIMS = sum(RIM)
FROM = (0, 7, 14)
CHUNKS = ((0, 2), (2, 4))

VM = pl.BlockSpec(memory_space=pltpu.VMEM)
SM = pl.BlockSpec(memory_space=pltpu.SMEM)
HB = pl.BlockSpec(memory_space=pltpu.HBM)
PARAMS = pltpu.CompilerParams(vmem_limit_bytes=24 << 20)


def pack_kernel(members, anc, state, out):
    me = lax.axis_index("dom")
    bits = jnp.int32(0)
    for j in range(anc.shape[0]):
        a = anc[j]
        hit = (a != j) & (a // members == me)
        bits = bits | jnp.where(hit, jnp.left_shift(1, a % members), 0)
    first = jnp.int32(members - 1)
    for k in reversed(range(members)):
        first = jnp.where((bits >> k) & 1 == 1, k, first)
    second = jnp.int32(members - 1)
    for k in reversed(range(members)):
        second = jnp.where(((bits >> k) & 1 == 1) & (k != first), k, second)
    for q, p in enumerate((first, second)):
        for f in range(state.shape[1]):
            for t in range(state.shape[2]):
                out[:, q, f, t] = state[p, f, t]


def coef_kernel(depth, coriolis, drag, above, below, out):
    tiles = out.shape[2]
    bands = depth.shape[0] // (tiles * SUB)
    for r in range(out.shape[1]):
        band, row = r // SUB - 1, r % SUB
        values = []
        for n, own in enumerate((depth, coriolis, drag)):
            ref, at = (above, n) if band < 0 else (below, n) if band == bands else (own, band)
            values.append(ref[pl.ds(at * tiles * SUB + row, tiles, stride=SUB), :])
        out[0, r] = (0.5 * DT) * values[0]
        out[1, r] = DT * values[1]
        out[2, r] = 1.0 / (1.0 + DT * values[2])


def pick_kernel(members, low, high, table, got, out):
    for d in range(out.shape[0]):
        for k in range(low, high):
            at = table[d * members + k]
            out[d, k - low] = got[at]


def prep_kernel(members, low, high, kept, routed, state, jitter, fields, top, bottom):
    kinds, rows, tiles = fields.shape[1:4]
    slab = kinds * rows
    for k in range(low, high):
        mine = kept[k] == 1
        for f in range(kinds):
            for r in range(rows):
                far = pl.ds(k * slab + f * rows + r, tiles, stride=members * slab)
                t = (k * kinds + f) * (rows // SUB) + r // SUB
                near = pl.ds(t * tiles * SUB + r % SUB, tiles, stride=SUB)
                value = jnp.where(mine, state[near, :], routed[far, :]) + jitter[near, :]
                fields[k - low, f, r] = value
                if r < RIM[f]:
                    top[k - low, FROM[f] + r] = value
                if r >= rows - RIM[f]:
                    bottom[k - low, FROM[f] + r - (rows - RIM[f])] = value


def step_kernel(size, fields, above, below, coef, *rest):
    out, *held = rest[-4:]
    kinds, rows, tiles = fields.shape[1:4]
    lane = lax.broadcasted_iota(jnp.int32, (tiles, LANES), 1)
    tile = lax.broadcasted_iota(jnp.int32, (tiles, LANES), 0)
    lane_first, lane_last = lane == 0, lane == LANES - 1
    wall_first = lane_first & (tile == 0)
    wall_last = lane_last & (tile == tiles - 1)
    half = 0.5 * DT

    def difference(x, edge):
        before = pltpu.roll(jnp.where(lane_last, pltpu.roll(x, 1, 0), x), 1, 1)
        after = pltpu.roll(jnp.where(lane_first, pltpu.roll(x, tiles - 1, 0), x), LANES - 1, 1)
        return jnp.where(wall_last, edge, after) - jnp.where(wall_first, edge, before)

    def const(n, r):
        return coef[n, r + DEEP]

    def particle(k, carry):
        def get(n, f, r):
            if n:
                return held[f][n - 1, r + DEEP]
            if r < 0:
                return above[k, FROM[f] + r + RIM[f]]
            if r >= rows:
                return below[k, FROM[f] + r - rows]
            return fields[k, f, r]

        def put(n, f, r, value):
            if n < STEPS or f == 0:
                held[f][n - 1, r + DEEP] = value
            if n == STEPS and 0 <= r < rows:
                at = pl.ds(r // SUB * tiles * SUB + r % SUB, tiles, stride=SUB)
                out[k, f, at, :] = value

        for n in range(STEPS):
            left = STEPS - 1 - n
            low_u, high_u = (1 - 2 * left, rows + 2 * left - 1) if left else (0, rows)
            for r in range(-(2 * left + 1), rows + 2 * left + 1):
                across = difference(const(0, r) * get(n, 1, r), 0.0)
                along = const(0, r + 1) * get(n, 2, r + 1) - const(0, r - 1) * get(n, 2, r - 1)
                put(n + 1, 0, r, get(n, 0, r) - (across + along))
            for r in range(-2 * left, rows + 2 * left):
                uu, vv, c, s = get(n, 1, r), get(n, 2, r), const(1, r), const(2, r)
                if low_u <= r < high_u:
                    here = get(n + 1, 0, r)
                    put(n + 1, 1, r, s * (uu + c * vv - half * difference(here, here)))
                along = get(n + 1, 0, r + 1) - get(n + 1, 0, r - 1)
                put(n + 1, 2, r, s * (vv - c * uu - half * along))
        return carry

    lax.fori_loop(0, size, particle, 0)


def local(ancestor, state, jitter, depth, coriolis, drag):
    members, kinds, rows, width = state.shape
    tiles, bands = width // LANES, rows // SUB
    blocks = lax.axis_size("dom")
    count = lax.axis_size("space")
    down = [(i, (i + 1) % count) for i in range(count)]
    up = [((i + 1) % count, i) for i in range(count)]
    me = lax.axis_index("dom")
    f32 = jnp.float32

    def tiled(x):
        x = x.reshape(x.shape[:-2] + (x.shape[-2] // SUB, SUB, tiles, LANES))
        return jnp.swapaxes(x, -3, -2)

    state_t, jitter_t = tiled(state), tiled(jitter)

    packed = pl.pallas_call(
        functools.partial(pack_kernel, members),
        in_specs=[SM, VM],
        out_specs=VM,
        out_shape=jax.ShapeDtypeStruct((tiles, CAP, kinds, bands, SUB, LANES), f32),
        compiler_params=PARAMS,
        name="pack",
    )(ancestor, state_t)
    pieces = lax.all_to_all(packed, "dom", 0, 0, tiled=True)
    pieces = pieces.reshape(blocks * CAP, kinds * rows, LANES)

    slot = jnp.arange(ancestor.shape[0], dtype=jnp.int32)
    moved = ancestor != slot
    donor = jnp.any((ancestor[:, None] == slot[None, :]) & moved[:, None], axis=0)
    same = (slot[:, None] // members == slot[None, :] // members) & (slot[:, None] < slot[None, :])
    rank = jnp.any(same & donor[:, None], axis=0).astype(jnp.int32)
    place = slot // members * CAP + rank
    table = jnp.sum(jnp.where(ancestor[:, None] == slot[None, :], place[None, :], 0), axis=1)
    kept = lax.dynamic_slice_in_dim(jnp.where(moved, 0, 1).astype(jnp.int32), me * members, members)

    raw = (depth, coriolis, drag)
    rim_above = lax.ppermute(jnp.stack([x[rows - DEEP :] for x in raw]), "space", down)
    rim_below = lax.ppermute(jnp.stack([x[:DEEP] for x in raw]), "space", up)
    coef = pl.pallas_call(
        coef_kernel,
        in_specs=[VM] * 5,
        out_specs=VM,
        out_shape=jax.ShapeDtypeStruct((3, rows + 2 * DEEP, tiles, LANES), f32),
        compiler_params=PARAMS,
        name="coef",
    )(
        *(tiled(x).reshape(rows * tiles, LANES) for x in raw),
        *(tiled(x).reshape(3 * DEEP * tiles, LANES) for x in (rim_above, rim_below)),
    )
    pieces, coef, table, kept = lax.optimization_barrier((pieces, coef, table, kept))

    chosen = pl.pallas_call(
        functools.partial(pick_kernel, members, 0, members),
        in_specs=[SM, VM],
        out_specs=VM,
        out_shape=jax.ShapeDtypeStruct((blocks, members, kinds * rows, LANES), f32),
        compiler_params=PARAMS,
        name="pick",
    )(table, pieces)
    routed = lax.all_to_all(chosen, "dom", 0, 0, tiled=True).reshape(-1, LANES)

    out = None
    chunks = []
    for low, high in CHUNKS:
        size = high - low
        rim = jax.ShapeDtypeStruct((size, RIMS, tiles, LANES), f32)
        fields, top, bottom = pl.pallas_call(
            functools.partial(prep_kernel, members, low, high),
            in_specs=[SM, VM, VM, VM],
            out_specs=(VM, VM, VM),
            out_shape=(jax.ShapeDtypeStruct((size, kinds, rows, tiles, LANES), f32), rim, rim),
            compiler_params=PARAMS,
            name="prep",
        )(kept, routed, state_t.reshape(-1, LANES), jitter_t.reshape(-1, LANES))
        above = lax.ppermute(bottom, "space", down)
        below = lax.ppermute(top, "space", up)
        chunks.append((fields, above, below))

    for (low, high), (fields, above, below) in zip(CHUNKS, chunks):
        size = high - low
        done = pl.BlockSpec((size, kinds, rows * tiles, LANES), lambda i, at=low // size: (at, 0, 0, 0))
        out = pl.pallas_call(
            functools.partial(step_kernel, size),
            grid=(1,),
            in_specs=[VM] * 4 + ([] if out is None else [HB]),
            out_specs=done,
            out_shape=jax.ShapeDtypeStruct((members, kinds, rows * tiles, LANES), f32),
            scratch_shapes=[pltpu.VMEM((STEPS, rows + 2 * DEEP, tiles, LANES), f32)] * 3,
            input_output_aliases={} if out is None else {4: 0},
            compiler_params=PARAMS,
            name="steps",
        )(fields, above, below, coef, *([] if out is None else [out]))
    out = out.reshape(members, kinds, bands, tiles, SUB, LANES)
    return jnp.swapaxes(out, -3, -2).reshape(state.shape)


def solution(mesh):
    placed = (
        P(),
        P("dom", None, "space", None),
        P("dom", None, "space", None),
        P("space", None),
        P("space", None),
        P("space", None),
    )
    return jax.shard_map(
        local, mesh=mesh, in_specs=placed, out_specs=P("dom", None, "space", None), check_vma=False
    )
```

```python
import functools

import jax
import jax.numpy as jnp
from jax import lax
from jax.experimental import pallas as pl
from jax.experimental.pallas import tpu as pltpu
from jax.sharding import PartitionSpec as P

STEPS = 4
CAP = 2
DT = 0.3
LANES = 128
SUB = 8
DEEP = 8
RIM = (7, 7, 8)
RIMS = sum(RIM)
FROM = (0, 7, 14)
CHUNKS = ((0, 2), (2, 4))

VM = pl.BlockSpec(memory_space=pltpu.VMEM)
SM = pl.BlockSpec(memory_space=pltpu.SMEM)
HB = pl.BlockSpec(memory_space=pltpu.HBM)
PARAMS = pltpu.CompilerParams(vmem_limit_bytes=24 << 20)


def pack_kernel(members, anc, state, out, sem):
    me = lax.axis_index("dom")
    bits = jnp.int32(0)
    for j in range(anc.shape[0]):
        a = anc[j]
        hit = (a != j) & (a // members == me)
        bits = bits | jnp.where(hit, jnp.left_shift(1, a % members), 0)
    first = jnp.int32(members - 1)
    for k in reversed(range(members)):
        first = jnp.where((bits >> k) & 1 == 1, k, first)
    second = jnp.int32(members - 1)
    for k in reversed(range(members)):
        second = jnp.where(((bits >> k) & 1 == 1) & (k != first), k, second)
    copies = []
    for q, p in enumerate((first, second)):
        for f in range(state.shape[1]):
            for t in range(state.shape[2]):
                copies.append(
                    pltpu.make_async_copy(state.at[p, f, t], out.at[:, q, f, t], sem.at[len(copies)])
                )
    for c in copies:
        c.start()
    for c in copies:
        c.wait()


def rim_kernel(depth, coriolis, drag, first, second, sem):
    toward = 1 - lax.axis_index("space") % 2
    last = depth.shape[0] - 1
    copies = []
    for n, ref in enumerate((depth, coriolis, drag)):
        for out, at in ((first, toward * last), (second, (1 - toward) * last)):
            copies.append(pltpu.make_async_copy(ref.at[at], out.at[n], sem.at[len(copies)]))
    for c in copies:
        c.start()
    for c in copies:
        c.wait()


def coef_kernel(depth, coriolis, drag, first, second, out):
    tiles = out.shape[2]
    bands = depth.shape[0] // (tiles * SUB)
    odd = lax.axis_index("space") % 2 == 1
    for r in range(out.shape[1]):
        band, row = r // SUB - 1, r % SUB
        values = []
        for n, own in enumerate((depth, coriolis, drag)):
            if 0 <= band < bands:
                values.append(own[pl.ds(band * tiles * SUB + row, tiles, stride=SUB), :])
            else:
                at = pl.ds(n * tiles * SUB + row, tiles, stride=SUB)
                values.append(jnp.where(odd == (band < 0), first[at, :], second[at, :]))
        out[0, r] = (0.5 * DT) * values[0]
        out[1, r] = DT * values[1]
        out[2, r] = 1.0 / (1.0 + DT * values[2])


def pick_kernel(members, low, high, table, got, out):
    for d in range(out.shape[0]):
        for k in range(low, high):
            at = table[d * members + k]
            out[d, k - low] = got[at]


def prep_kernel(members, low, high, kept, routed, state, jitter, fields, first, second):
    kinds, rows, tiles = fields.shape[1:4]
    slab = kinds * rows
    odd = lax.axis_index("space") % 2 == 1
    for k in range(low, high):
        mine = kept[k] == 1
        for f in range(kinds):
            values = []
            for r in range(rows):
                far = pl.ds(k * slab + f * rows + r, tiles, stride=members * slab)
                t = (k * kinds + f) * (rows // SUB) + r // SUB
                near = pl.ds(t * tiles * SUB + r % SUB, tiles, stride=SUB)
                value = jnp.where(mine, state[near, :], routed[far, :]) + jitter[near, :]
                fields[k - low, f, r] = value
                values.append(value)
            for r in range(RIM[f]):
                top, bottom = values[r], values[rows - RIM[f] + r]
                first[k - low, FROM[f] + r] = jnp.where(odd, top, bottom)
                second[k - low, FROM[f] + r] = jnp.where(odd, bottom, top)


def step_kernel(size, fields, first, second, coef, *rest):
    out, *held = rest[-4:]
    kinds, rows, tiles = fields.shape[1:4]
    lane = lax.broadcasted_iota(jnp.int32, (tiles, LANES), 1)
    tile = lax.broadcasted_iota(jnp.int32, (tiles, LANES), 0)
    lane_first, lane_last = lane == 0, lane == LANES - 1
    wall_first = lane_first & (tile == 0)
    wall_last = lane_last & (tile == tiles - 1)
    half = 0.5 * DT
    odd = lax.axis_index("space") % 2 == 1

    def difference(x, edge):
        before = pltpu.roll(jnp.where(lane_last, pltpu.roll(x, 1, 0), x), 1, 1)
        after = pltpu.roll(jnp.where(lane_first, pltpu.roll(x, tiles - 1, 0), x), LANES - 1, 1)
        return jnp.where(wall_last, edge, after) - jnp.where(wall_first, edge, before)

    def const(n, r):
        return coef[n, r + DEEP]

    def particle(k, carry):
        def get(n, f, r):
            if n:
                return held[f][n - 1, r + DEEP]
            if 0 <= r < rows:
                return fields[k, f, r]
            at = FROM[f] + (r + RIM[f] if r < 0 else r - rows)
            return jnp.where(odd == (r < 0), first[k, at], second[k, at])

        def put(n, f, r, value):
            if n < STEPS or f == 0:
                held[f][n - 1, r + DEEP] = value
            if n == STEPS and 0 <= r < rows:
                at = pl.ds(r // SUB * tiles * SUB + r % SUB, tiles, stride=SUB)
                out[k, f, at, :] = value

        for n in range(STEPS):
            left = STEPS - 1 - n
            low_u, high_u = (1 - 2 * left, rows + 2 * left - 1) if left else (0, rows)
            for r in range(-(2 * left + 1), rows + 2 * left + 1):
                across = difference(const(0, r) * get(n, 1, r), 0.0)
                along = const(0, r + 1) * get(n, 2, r + 1) - const(0, r - 1) * get(n, 2, r - 1)
                put(n + 1, 0, r, get(n, 0, r) - (across + along))
            for r in range(-2 * left, rows + 2 * left):
                uu, vv, c, s = get(n, 1, r), get(n, 2, r), const(1, r), const(2, r)
                if low_u <= r < high_u:
                    here = get(n + 1, 0, r)
                    put(n + 1, 1, r, s * (uu + c * vv - half * difference(here, here)))
                along = get(n + 1, 0, r + 1) - get(n + 1, 0, r - 1)
                put(n + 1, 2, r, s * (vv - c * uu - half * along))
        return carry

    lax.fori_loop(0, size, particle, 0)


def local(ancestor, state, jitter, depth, coriolis, drag):
    members, kinds, rows, width = state.shape
    tiles, bands = width // LANES, rows // SUB
    blocks = lax.axis_size("dom")
    count = lax.axis_size("space")
    swap_first = [(i, i ^ 1) for i in range(count)]
    swap_second = [(i, (i + 2 * (i % 2) - 1) % count) for i in range(count)]
    me = lax.axis_index("dom")
    f32 = jnp.float32

    def tiled(x):
        x = x.reshape(x.shape[:-2] + (x.shape[-2] // SUB, SUB, tiles, LANES))
        return jnp.swapaxes(x, -3, -2)

    state_t, jitter_t = tiled(state), tiled(jitter)

    packed = pl.pallas_call(
        functools.partial(pack_kernel, members),
        in_specs=[SM, HB],
        out_specs=HB,
        out_shape=jax.ShapeDtypeStruct((tiles, CAP, kinds, bands, SUB, LANES), f32),
        scratch_shapes=[pltpu.SemaphoreType.DMA((CAP * kinds * bands,))],
        compiler_params=PARAMS,
        name="pack",
    )(ancestor, pltpu.with_memory_space_constraint(state_t, pltpu.HBM))
    pieces = lax.all_to_all(packed, "dom", 0, 0, tiled=True)
    pieces = pieces.reshape(blocks * CAP, kinds * rows, LANES)

    slot = jnp.arange(ancestor.shape[0], dtype=jnp.int32)
    moved = ancestor != slot
    donor = jnp.any((ancestor[:, None] == slot[None, :]) & moved[:, None], axis=0)
    same = (slot[:, None] // members == slot[None, :] // members) & (slot[:, None] < slot[None, :])
    rank = jnp.any(same & donor[:, None], axis=0).astype(jnp.int32)
    place = slot // members * CAP + rank
    table = jnp.sum(jnp.where(ancestor[:, None] == slot[None, :], place[None, :], 0), axis=1)
    kept = lax.dynamic_slice_in_dim(jnp.where(moved, 0, 1).astype(jnp.int32), me * members, members)

    raw = (depth, coriolis, drag)
    rim = jax.ShapeDtypeStruct((3, tiles, SUB, LANES), f32)
    rims = pl.pallas_call(
        rim_kernel,
        in_specs=[HB] * 3,
        out_specs=(VM, VM),
        out_shape=(rim, rim),
        scratch_shapes=[pltpu.SemaphoreType.DMA((6,))],
        compiler_params=PARAMS,
        name="rims",
    )(*(pltpu.with_memory_space_constraint(tiled(x), pltpu.HBM) for x in raw))
    rims = (lax.ppermute(rims[0], "space", swap_first), lax.ppermute(rims[1], "space", swap_second))
    coef = pl.pallas_call(
        coef_kernel,
        in_specs=[VM] * 5,
        out_specs=VM,
        out_shape=jax.ShapeDtypeStruct((3, rows + 2 * DEEP, tiles, LANES), f32),
        compiler_params=PARAMS,
        name="coef",
    )(
        *(tiled(x).reshape(rows * tiles, LANES) for x in raw),
        *(x.reshape(3 * tiles * SUB, LANES) for x in rims),
    )
    pieces, coef, table, kept = lax.optimization_barrier((pieces, coef, table, kept))

    chosen = pl.pallas_call(
        functools.partial(pick_kernel, members, 0, members),
        in_specs=[SM, VM],
        out_specs=VM,
        out_shape=jax.ShapeDtypeStruct((blocks, members, kinds * rows, LANES), f32),
        compiler_params=PARAMS,
        name="pick",
    )(table, pieces)
    routed = lax.all_to_all(chosen, "dom", 0, 0, tiled=True).reshape(-1, LANES)

    out = None
    chunks = []
    for low, high in CHUNKS:
        size = high - low
        rim = jax.ShapeDtypeStruct((size, RIMS, tiles, LANES), f32)
        fields, first, second = pl.pallas_call(
            functools.partial(prep_kernel, members, low, high),
            in_specs=[SM, VM, VM, VM],
            out_specs=(VM, VM, VM),
            out_shape=(jax.ShapeDtypeStruct((size, kinds, rows, tiles, LANES), f32), rim, rim),
            compiler_params=PARAMS,
            name="prep",
        )(kept, routed, state_t.reshape(-1, LANES), jitter_t.reshape(-1, LANES))
        first = lax.ppermute(first, "space", swap_first)
        second = lax.ppermute(second, "space", swap_second)
        chunks.append((fields, first, second))

    for (low, high), (fields, first, second) in zip(CHUNKS, chunks):
        size = high - low
        done = pl.BlockSpec((size, kinds, rows * tiles, LANES), lambda i, at=low // size: (at, 0, 0, 0))
        out = pl.pallas_call(
            functools.partial(step_kernel, size),
            grid=(1,),
            in_specs=[VM] * 4 + ([] if out is None else [HB]),
            out_specs=done,
            out_shape=jax.ShapeDtypeStruct((members, kinds, rows * tiles, LANES), f32),
            scratch_shapes=[pltpu.VMEM((STEPS, rows + 2 * DEEP, tiles, LANES), f32)] * 3,
            input_output_aliases={} if out is None else {4: 0},
            compiler_params=PARAMS,
            name="steps",
        )(fields, first, second, coef, *([] if out is None else [out]))
    out = out.reshape(members, kinds, bands, tiles, SUB, LANES)
    return jnp.swapaxes(out, -3, -2).reshape(state.shape)


def solution(mesh):
    placed = (
        P(),
        P("dom", None, "space", None),
        P("dom", None, "space", None),
        P("space", None),
        P("space", None),
        P("space", None),
    )
    return jax.shard_map(
        local, mesh=mesh, in_specs=placed, out_specs=P("dom", None, "space", None), check_vma=False
    )
```

```python
import functools

import jax
import jax.numpy as jnp
from jax import lax
from jax.experimental import pallas as pl
from jax.experimental.pallas import tpu as pltpu
from jax.sharding import PartitionSpec as P

STEPS = 4
CAP = 2
DT = 0.3
LANES = 128
SUB = 8
DEEP = 8
RIM = (7, 7, 8)
RIMS = sum(RIM)
FROM = (0, 7, 14)
CHUNKS = {2: (1, 1), 3: (2, 1), 4: (2, 2)}

VM = pl.BlockSpec(memory_space=pltpu.VMEM)
SM = pl.BlockSpec(memory_space=pltpu.SMEM)
HB = pl.BlockSpec(memory_space=pltpu.HBM)
PARAMS = pltpu.CompilerParams(vmem_limit_bytes=24 << 20)


def pack_kernel(members, anc, state, out, sem):
    me = lax.axis_index("dom")
    bits = jnp.int32(0)
    for j in range(anc.shape[0]):
        a = anc[j]
        hit = (a != j) & (a // members == me)
        bits = bits | jnp.where(hit, jnp.left_shift(1, a % members), 0)
    first = jnp.int32(members - 1)
    for k in reversed(range(members)):
        first = jnp.where((bits >> k) & 1 == 1, k, first)
    second = jnp.int32(members - 1)
    for k in reversed(range(members)):
        second = jnp.where(((bits >> k) & 1 == 1) & (k != first), k, second)
    copies = []
    for q, p in enumerate((first, second)):
        for f in range(state.shape[1]):
            for t in range(state.shape[2]):
                copies.append(
                    pltpu.make_async_copy(state.at[p, f, t], out.at[:, q, f, t], sem.at[len(copies)])
                )
    for c in copies:
        c.start()
    for c in copies:
        c.wait()


def rim_kernel(depth, coriolis, drag, first, second, sem):
    toward = 1 - lax.axis_index("space") % 2
    last = depth.shape[0] - 1
    copies = []
    for n, ref in enumerate((depth, coriolis, drag)):
        for out, at in ((first, toward * last), (second, (1 - toward) * last)):
            copies.append(pltpu.make_async_copy(ref.at[at], out.at[n], sem.at[len(copies)]))
    for c in copies:
        c.start()
    for c in copies:
        c.wait()


def coef_kernel(depth, coriolis, drag, first, second, out):
    tiles = out.shape[2]
    bands = depth.shape[0] // (tiles * SUB)
    odd = lax.axis_index("space") % 2 == 1
    for r in range(out.shape[1]):
        band, row = r // SUB - 1, r % SUB
        values = []
        for n, own in enumerate((depth, coriolis, drag)):
            if 0 <= band < bands:
                values.append(own[pl.ds(band * tiles * SUB + row, tiles, stride=SUB), :])
            else:
                at = pl.ds(n * tiles * SUB + row, tiles, stride=SUB)
                values.append(jnp.where(odd == (band < 0), first[at, :], second[at, :]))
        out[0, r] = (0.5 * DT) * values[0]
        out[1, r] = DT * values[1]
        out[2, r] = 1.0 / (1.0 + DT * values[2])


def pick_kernel(members, table, got, out):
    size = out.shape[1]
    for d in range(out.shape[0]):
        for k in range(size):
            out[d, k] = got[table[(d + 1) * members - size + k]]


def prep_kernel(low, order, gone, state, jitter, *rest):
    *routed, fields, first, second = rest
    size, kinds, rows, tiles = fields.shape[:4]
    slab = kinds * rows
    odd = lax.axis_index("space") % 2 == 1
    for k in range(size):
        slot = order[low + k]
        if routed:
            ref, = routed
            late = ref.shape[0] // (tiles * slab)
            at = low + k - (order.shape[0] - late)
            mine = gone[low + k] == 0
        for f in range(kinds):
            values = []
            for r in range(rows):
                near = pl.ds((f * (rows // SUB) + r // SUB) * tiles * SUB + r % SUB, tiles, stride=SUB)
                value = state[slot, near, :]
                if routed:
                    far = ref[pl.ds(at * slab + f * rows + r, tiles, stride=late * slab), :]
                    value = jnp.where(mine, value, far)
                value = value + jitter[slot, near, :]
                fields[k, f, r] = value
                values.append(value)
            for r in range(RIM[f]):
                top, bottom = values[r], values[rows - RIM[f] + r]
                first[k, FROM[f] + r] = jnp.where(odd, top, bottom)
                second[k, FROM[f] + r] = jnp.where(odd, bottom, top)


def step_kernel(low, order, fields, first, second, coef, *rest):
    whole, out, sem, *held = rest[-6:]
    size, kinds, rows, tiles = fields.shape[:4]
    lane = lax.broadcasted_iota(jnp.int32, (tiles, LANES), 1)
    tile = lax.broadcasted_iota(jnp.int32, (tiles, LANES), 0)
    lane_first, lane_last = lane == 0, lane == LANES - 1
    wall_first = lane_first & (tile == 0)
    wall_last = lane_last & (tile == tiles - 1)
    half = 0.5 * DT
    odd = lax.axis_index("space") % 2 == 1

    def difference(x, edge):
        before = pltpu.roll(jnp.where(lane_last, pltpu.roll(x, 1, 0), x), 1, 1)
        after = pltpu.roll(jnp.where(lane_first, pltpu.roll(x, tiles - 1, 0), x), LANES - 1, 1)
        return jnp.where(wall_last, edge, after) - jnp.where(wall_first, edge, before)

    def const(n, r):
        return coef[n, r + DEEP]

    def particle(k, carry):
        def get(n, f, r):
            if n:
                return held[f][n - 1, r + DEEP]
            if 0 <= r < rows:
                return fields[k, f, r]
            at = FROM[f] + (r + RIM[f] if r < 0 else r - rows)
            return jnp.where(odd == (r < 0), first[k, at], second[k, at])

        def put(n, f, r, value):
            if n < STEPS or f == 0:
                held[f][n - 1, r + DEEP] = value
            if n == STEPS and 0 <= r < rows:
                at = pl.ds(r // SUB * tiles * SUB + r % SUB, tiles, stride=SUB)
                out[k, f, at, :] = value

        for n in range(STEPS):
            left = STEPS - 1 - n
            low_u, high_u = (1 - 2 * left, rows + 2 * left - 1) if left else (0, rows)
            for r in range(-(2 * left + 1), rows + 2 * left + 1):
                across = difference(const(0, r) * get(n, 1, r), 0.0)
                along = const(0, r + 1) * get(n, 2, r + 1) - const(0, r - 1) * get(n, 2, r - 1)
                put(n + 1, 0, r, get(n, 0, r) - (across + along))
            for r in range(-2 * left, rows + 2 * left):
                uu, vv, c, s = get(n, 1, r), get(n, 2, r), const(1, r), const(2, r)
                if low_u <= r < high_u:
                    here = get(n + 1, 0, r)
                    put(n + 1, 1, r, s * (uu + c * vv - half * difference(here, here)))
                along = get(n + 1, 0, r + 1) - get(n + 1, 0, r - 1)
                put(n + 1, 2, r, s * (vv - c * uu - half * along))
        copy_out(k).start()
        return carry

    def copy_out(k):
        return pltpu.make_async_copy(out.at[k], whole.at[order[low + k]], sem.at[k])

    lax.fori_loop(0, size, particle, 0)
    for k in range(size):
        copy_out(k).wait()


def local(ancestor, state, jitter, depth, coriolis, drag):
    members, kinds, rows, width = state.shape
    tiles, bands = width // LANES, rows // SUB
    blocks = lax.axis_size("dom")
    count = lax.axis_size("space")
    swap_first = [(i, i ^ 1) for i in range(count)]
    swap_second = [(i, (i + 2 * (i % 2) - 1) % count) for i in range(count)]
    me = lax.axis_index("dom")
    f32 = jnp.float32

    def tiled(x):
        x = x.reshape(x.shape[:-2] + (x.shape[-2] // SUB, SUB, tiles, LANES))
        return jnp.swapaxes(x, -3, -2)

    state_t, jitter_t = tiled(state), tiled(jitter)

    packed = pl.pallas_call(
        functools.partial(pack_kernel, members),
        in_specs=[SM, HB],
        out_specs=VM,
        out_shape=jax.ShapeDtypeStruct((tiles, CAP, kinds, bands, SUB, LANES), f32),
        scratch_shapes=[pltpu.SemaphoreType.DMA((CAP * kinds * bands,))],
        compiler_params=PARAMS,
        name="pack",
    )(ancestor, pltpu.with_memory_space_constraint(state_t, pltpu.HBM))
    pieces = lax.all_to_all(packed, "dom", 0, 0, tiled=True)
    pieces = pieces.reshape(blocks * CAP, kinds * rows, LANES)

    slot = jnp.arange(ancestor.shape[0], dtype=jnp.int32)
    moved = ancestor != slot
    same = slot[:, None] // members == slot[None, :] // members
    donor = jnp.any((ancestor[:, None] == slot[None, :]) & moved[:, None], axis=0)
    rank = jnp.any(same & (slot[:, None] < slot[None, :]) & donor[:, None], axis=0).astype(jnp.int32)
    place = slot // members * CAP + rank
    source = jnp.sum(jnp.where(ancestor[:, None] == slot[None, :], place[None, :], 0), axis=1)

    rated = slot + jnp.where(moved, ancestor.shape[0], 0)
    turn = jnp.sum((same & (rated[:, None] < rated[None, :])).astype(jnp.int32), axis=0)
    seat = slot // members * members + turn
    hit = seat[None, :] == slot[:, None]
    table = jnp.sum(jnp.where(hit, source[None, :], 0), axis=1)
    pair = jnp.sum(jnp.where(hit, slot[None, :] % members + members * moved[None, :], 0), axis=1)
    pair = lax.dynamic_slice_in_dim(pair, me * members, members)
    order, gone = pair % members, pair // members
    most = jnp.max(jnp.sum((same & moved[:, None]).astype(jnp.int32), axis=0))

    raw = (depth, coriolis, drag)
    rim = jax.ShapeDtypeStruct((3, tiles, SUB, LANES), f32)
    rims = pl.pallas_call(
        rim_kernel,
        in_specs=[HB] * 3,
        out_specs=(VM, VM),
        out_shape=(rim, rim),
        scratch_shapes=[pltpu.SemaphoreType.DMA((6,))],
        compiler_params=PARAMS,
        name="rims",
    )(*(pltpu.with_memory_space_constraint(tiled(x), pltpu.HBM) for x in raw))
    rims = (lax.ppermute(rims[0], "space", swap_first), lax.ppermute(rims[1], "space", swap_second))
    coef = pl.pallas_call(
        coef_kernel,
        in_specs=[VM] * 5,
        out_specs=VM,
        out_shape=jax.ShapeDtypeStruct((3, rows + 2 * DEEP, tiles, LANES), f32),
        compiler_params=PARAMS,
        name="coef",
    )(
        *(tiled(x).reshape(rows * tiles, LANES) for x in raw),
        *(x.reshape(3 * tiles * SUB, LANES) for x in rims),
    )
    sides = (members, kinds * rows * tiles, LANES)
    state_t, jitter_t = state_t.reshape(sides), jitter_t.reshape(sides)

    def prepared(low, size, order, gone, routed):
        rim = jax.ShapeDtypeStruct((size, RIMS, tiles, LANES), f32)
        fields, first, second = pl.pallas_call(
            functools.partial(prep_kernel, low),
            in_specs=[SM, SM] + [VM] * (2 + len(routed)),
            out_specs=(VM, VM, VM),
            out_shape=(jax.ShapeDtypeStruct((size, kinds, rows, tiles, LANES), f32), rim, rim),
            compiler_params=PARAMS,
            name="prep",
        )(order, gone, state_t, jitter_t, *routed)
        first = lax.ppermute(first, "space", swap_first)
        second = lax.ppermute(second, "space", swap_second)
        return fields, first, second

    def stepped(low, size, order, parts, coef, out):
        return pl.pallas_call(
            functools.partial(step_kernel, low),
            in_specs=[SM] + [VM] * 4 + [HB] * len(out),
            out_specs=HB,
            out_shape=jax.ShapeDtypeStruct((members, kinds, rows * tiles, LANES), f32),
            scratch_shapes=[
                pltpu.VMEM((size, kinds, rows * tiles, LANES), f32),
                pltpu.SemaphoreType.DMA((size,)),
            ]
            + [pltpu.VMEM((STEPS, rows + 2 * DEEP, tiles, LANES), f32)] * 3,
            input_output_aliases={5: 0} if out else {},
            compiler_params=PARAMS,
            name="steps",
        )(order, *parts, coef, *out)

    def rest(late, pieces, coef, table, order, gone):
        early = members - late
        chosen = pl.pallas_call(
            functools.partial(pick_kernel, members),
            in_specs=[SM, VM],
            out_specs=VM,
            out_shape=jax.ShapeDtypeStruct((blocks, late, kinds * rows, LANES), f32),
            compiler_params=PARAMS,
            name="pick",
        )(table, pieces)
        routed = lax.all_to_all(chosen, "dom", 0, 0, tiled=True).reshape(-1, LANES)
        out = []
        if early:
            parts = prepared(0, early, order, gone, ())
            out = [stepped(0, early, order, parts, coef, out)]
        chunks = []
        for size in CHUNKS[late]:
            chunks.append((early, size, prepared(early, size, order, gone, (routed,))))
            early += size
        for low, size, parts in chunks:
            out = [stepped(low, size, order, parts, coef, out)]
        return out[0]

    args = lax.optimization_barrier((pieces, coef, table, order, gone))
    sizes = sorted(CHUNKS)
    which = jnp.clip(most - sizes[0], 0, len(sizes) - 1)
    out = lax.switch(which, [functools.partial(rest, size) for size in sizes], *args)
    out = out.reshape(members, kinds, bands, tiles, SUB, LANES)
    return jnp.swapaxes(out, -3, -2).reshape(state.shape)


def solution(mesh):
    placed = (
        P(),
        P("dom", None, "space", None),
        P("dom", None, "space", None),
        P("space", None),
        P("space", None),
        P("space", None),
    )
    return jax.shard_map(
        local, mesh=mesh, in_specs=placed, out_specs=P("dom", None, "space", None), check_vma=False
    )
```

```python
import functools

import jax
import jax.numpy as jnp
from jax import lax
from jax.experimental import pallas as pl
from jax.experimental.pallas import tpu as pltpu
from jax.sharding import PartitionSpec as P

STEPS = 4
CAP = 2
DT = 0.3
LANES = 128
SUB = 8
DEEP = 8
RIM = (7, 7, 8)
RIMS = sum(RIM)
FROM = (0, 7, 14)
CHUNKS = (2, 1, 1)
SIZES = (2, 3, 4)

VM = pl.BlockSpec(memory_space=pltpu.VMEM)
SM = pl.BlockSpec(memory_space=pltpu.SMEM)
HB = pl.BlockSpec(memory_space=pltpu.HBM)
PARAMS = pltpu.CompilerParams(vmem_limit_bytes=24 << 20)


def pack_kernel(members, anc, state, out, held, sem):
    me = lax.axis_index("dom")
    bits = jnp.int32(0)
    for j in range(anc.shape[0]):
        a = anc[j]
        hit = (a != j) & (a // members == me)
        bits = bits | jnp.where(hit, jnp.left_shift(1, a % members), 0)
    first = jnp.int32(members - 1)
    for k in reversed(range(members)):
        first = jnp.where((bits >> k) & 1 == 1, k, first)
    second = jnp.int32(members - 1)
    for k in reversed(range(members)):
        second = jnp.where(((bits >> k) & 1 == 1) & (k != first), k, second)
    into, onto = [], []
    for q, p in enumerate((first, second)):
        for f in range(state.shape[1]):
            for t in range(state.shape[2]):
                n = len(into)
                into.append(pltpu.make_async_copy(state.at[p, f, t], held.at[n], sem.at[0, n]))
                onto.append(pltpu.make_async_copy(held.at[n], out.at[:, q, f, t], sem.at[1, n]))
    for c in into:
        c.start()
    for i, o in zip(into, onto):
        i.wait()
        o.start()
    for o in onto:
        o.wait()


def rim_kernel(depth, coriolis, drag, first, second, sem):
    toward = 1 - lax.axis_index("space") % 2
    last = depth.shape[0] - 1
    copies = []
    for n, ref in enumerate((depth, coriolis, drag)):
        for out, at in ((first, toward * last), (second, (1 - toward) * last)):
            copies.append(pltpu.make_async_copy(ref.at[at], out.at[n], sem.at[len(copies)]))
    for c in copies:
        c.start()
    for c in copies:
        c.wait()


def coef_kernel(depth, coriolis, drag, first, second, out):
    tiles = out.shape[2]
    bands = depth.shape[0] // (tiles * SUB)
    odd = lax.axis_index("space") % 2 == 1
    for r in range(out.shape[1]):
        band, row = r // SUB - 1, r % SUB
        values = []
        for n, own in enumerate((depth, coriolis, drag)):
            if 0 <= band < bands:
                values.append(own[pl.ds(band * tiles * SUB + row, tiles, stride=SUB), :])
            else:
                at = pl.ds(n * tiles * SUB + row, tiles, stride=SUB)
                values.append(jnp.where(odd == (band < 0), first[at, :], second[at, :]))
        out[0, r] = (0.5 * DT) * values[0]
        out[1, r] = DT * values[1]
        out[2, r] = 1.0 / (1.0 + DT * values[2])


def pick_kernel(members, table, got, out):
    size = out.shape[1]
    for d in range(out.shape[0]):
        for k in range(size):
            out[d, k] = got[table[(d + 1) * members - size + k]]


def base_kernel(order, gone, state, jitter, out):
    members, kinds, rows, tiles = out.shape[:4]
    for k in range(members):
        slot = order[k]
        mine = gone[k] == 0
        for f in range(kinds):
            for r in range(rows):
                near = pl.ds((f * (rows // SUB) + r // SUB) * tiles * SUB + r % SUB, tiles, stride=SUB)
                out[k, f, r] = jnp.where(mine, state[slot, near, :], 0.0) + jitter[slot, near, :]


def prep_kernel(low, gone, base, routed, fields, first, second):
    size, kinds, rows, tiles = fields.shape[:4]
    slab = kinds * rows
    late = routed.shape[0] // (tiles * slab)
    odd = lax.axis_index("space") % 2 == 1
    for k in range(size):
        at = low + k - (base.shape[0] - late)
        mine = gone[low + k] == 0
        for f in range(kinds):
            values = []
            for r in range(rows):
                value = base[low + k, f, r]
                if at >= 0:
                    far = routed[pl.ds(at * slab + f * rows + r, tiles, stride=late * slab), :]
                    value = jnp.where(mine, value, value + far)
                fields[k, f, r] = value
                values.append(value)
            for r in range(RIM[f]):
                top, bottom = values[r], values[rows - RIM[f] + r]
                first[k, FROM[f] + r] = jnp.where(odd, top, bottom)
                second[k, FROM[f] + r] = jnp.where(odd, bottom, top)


def step_kernel(low, order, fields, first, second, coef, *rest):
    whole, out, sem, *held = rest[-6:]
    size, kinds, rows, tiles = fields.shape[:4]
    lane = lax.broadcasted_iota(jnp.int32, (tiles, LANES), 1)
    tile = lax.broadcasted_iota(jnp.int32, (tiles, LANES), 0)
    lane_first, lane_last = lane == 0, lane == LANES - 1
    wall_first = lane_first & (tile == 0)
    wall_last = lane_last & (tile == tiles - 1)
    half = 0.5 * DT
    odd = lax.axis_index("space") % 2 == 1

    def difference(x, edge):
        before = pltpu.roll(jnp.where(lane_last, pltpu.roll(x, 1, 0), x), 1, 1)
        after = pltpu.roll(jnp.where(lane_first, pltpu.roll(x, tiles - 1, 0), x), LANES - 1, 1)
        return jnp.where(wall_last, edge, after) - jnp.where(wall_first, edge, before)

    def const(n, r):
        return coef[n, r + DEEP]

    def particle(k, carry):
        def get(n, f, r):
            if n:
                return held[f][n - 1, r + DEEP]
            if 0 <= r < rows:
                return fields[k, f, r]
            at = FROM[f] + (r + RIM[f] if r < 0 else r - rows)
            return jnp.where(odd == (r < 0), first[k, at], second[k, at])

        def put(n, f, r, value):
            if n < STEPS or f == 0:
                held[f][n - 1, r + DEEP] = value
            if n == STEPS and 0 <= r < rows:
                at = pl.ds(r // SUB * tiles * SUB + r % SUB, tiles, stride=SUB)
                out[k, f, at, :] = value

        for n in range(STEPS):
            left = STEPS - 1 - n
            low_u, high_u = (1 - 2 * left, rows + 2 * left - 1) if left else (0, rows)
            for r in range(-(2 * left + 1), rows + 2 * left + 1):
                across = difference(const(0, r) * get(n, 1, r), 0.0)
                along = const(0, r + 1) * get(n, 2, r + 1) - const(0, r - 1) * get(n, 2, r - 1)
                put(n + 1, 0, r, get(n, 0, r) - (across + along))
            for r in range(-2 * left, rows + 2 * left):
                uu, vv, c, s = get(n, 1, r), get(n, 2, r), const(1, r), const(2, r)
                if low_u <= r < high_u:
                    here = get(n + 1, 0, r)
                    put(n + 1, 1, r, s * (uu + c * vv - half * difference(here, here)))
                along = get(n + 1, 0, r + 1) - get(n + 1, 0, r - 1)
                put(n + 1, 2, r, s * (vv - c * uu - half * along))
        copy_out(k).start()
        return carry

    def copy_out(k):
        return pltpu.make_async_copy(out.at[k], whole.at[order[low + k]], sem.at[k])

    lax.fori_loop(0, size, particle, 0)
    for k in range(size):
        copy_out(k).wait()


def local(ancestor, state, jitter, depth, coriolis, drag):
    members, kinds, rows, width = state.shape
    tiles, bands = width // LANES, rows // SUB
    blocks = lax.axis_size("dom")
    count = lax.axis_size("space")
    swap_first = [(i, i ^ 1) for i in range(count)]
    swap_second = [(i, (i + 2 * (i % 2) - 1) % count) for i in range(count)]
    me = lax.axis_index("dom")
    f32 = jnp.float32

    def tiled(x):
        x = x.reshape(x.shape[:-2] + (x.shape[-2] // SUB, SUB, tiles, LANES))
        return jnp.swapaxes(x, -3, -2)

    state_t, jitter_t = tiled(state), tiled(jitter)

    packed = pl.pallas_call(
        functools.partial(pack_kernel, members),
        in_specs=[SM, HB],
        out_specs=HB,
        out_shape=jax.ShapeDtypeStruct((tiles, CAP, kinds, bands, SUB, LANES), f32),
        scratch_shapes=[
            pltpu.VMEM((CAP * kinds * bands, tiles, SUB, LANES), f32),
            pltpu.SemaphoreType.DMA((2, CAP * kinds * bands)),
        ],
        compiler_params=PARAMS,
        name="pack",
    )(ancestor, pltpu.with_memory_space_constraint(state_t, pltpu.HBM))
    pieces = lax.all_to_all(packed, "dom", 0, 0, tiled=True)
    pieces = pieces.reshape(blocks * CAP, kinds * rows, LANES)

    slot = jnp.arange(ancestor.shape[0], dtype=jnp.int32)
    moved = ancestor != slot
    same = slot[:, None] // members == slot[None, :] // members
    donor = jnp.any((ancestor[:, None] == slot[None, :]) & moved[:, None], axis=0)
    rank = jnp.any(same & (slot[:, None] < slot[None, :]) & donor[:, None], axis=0).astype(jnp.int32)
    place = slot // members * CAP + rank
    source = jnp.sum(jnp.where(ancestor[:, None] == slot[None, :], place[None, :], 0), axis=1)

    rated = slot + jnp.where(moved, ancestor.shape[0], 0)
    turn = jnp.sum((same & (rated[:, None] < rated[None, :])).astype(jnp.int32), axis=0)
    seat = slot // members * members + turn
    hit = seat[None, :] == slot[:, None]
    table = jnp.sum(jnp.where(hit, source[None, :], 0), axis=1)
    pair = jnp.sum(jnp.where(hit, slot[None, :] % members + members * moved[None, :], 0), axis=1)
    pair = lax.dynamic_slice_in_dim(pair, me * members, members)
    order, gone = pair % members, pair // members
    most = jnp.max(jnp.sum((same & moved[:, None]).astype(jnp.int32), axis=0))

    raw = (depth, coriolis, drag)
    rim = jax.ShapeDtypeStruct((3, tiles, SUB, LANES), f32)
    rims = pl.pallas_call(
        rim_kernel,
        in_specs=[HB] * 3,
        out_specs=(VM, VM),
        out_shape=(rim, rim),
        scratch_shapes=[pltpu.SemaphoreType.DMA((6,))],
        compiler_params=PARAMS,
        name="rims",
    )(*(pltpu.with_memory_space_constraint(tiled(x), pltpu.HBM) for x in raw))
    rims = (lax.ppermute(rims[0], "space", swap_first), lax.ppermute(rims[1], "space", swap_second))
    coef = pl.pallas_call(
        coef_kernel,
        in_specs=[VM] * 5,
        out_specs=VM,
        out_shape=jax.ShapeDtypeStruct((3, rows + 2 * DEEP, tiles, LANES), f32),
        compiler_params=PARAMS,
        name="coef",
    )(
        *(tiled(x).reshape(rows * tiles, LANES) for x in raw),
        *(x.reshape(3 * tiles * SUB, LANES) for x in rims),
    )
    sides = (members, kinds * rows * tiles, LANES)
    state_t, jitter_t = state_t.reshape(sides), jitter_t.reshape(sides)

    base = pl.pallas_call(
        base_kernel,
        in_specs=[SM, SM, VM, VM],
        out_specs=VM,
        out_shape=jax.ShapeDtypeStruct((members, kinds, rows, tiles, LANES), f32),
        compiler_params=PARAMS,
        name="base",
    )(order, gone, state_t, jitter_t)

    def prepared(low, size, gone, base, routed):
        rim = jax.ShapeDtypeStruct((size, RIMS, tiles, LANES), f32)
        fields, first, second = pl.pallas_call(
            functools.partial(prep_kernel, low),
            in_specs=[SM, VM, VM],
            out_specs=(VM, VM, VM),
            out_shape=(jax.ShapeDtypeStruct((size, kinds, rows, tiles, LANES), f32), rim, rim),
            compiler_params=PARAMS,
            name="prep",
        )(gone, base, routed)
        first = lax.ppermute(first, "space", swap_first)
        second = lax.ppermute(second, "space", swap_second)
        return fields, first, second

    def stepped(low, size, order, parts, coef, out):
        return pl.pallas_call(
            functools.partial(step_kernel, low),
            in_specs=[SM] + [VM] * 4 + [HB] * len(out),
            out_specs=HB,
            out_shape=jax.ShapeDtypeStruct((members, kinds, rows * tiles, LANES), f32),
            scratch_shapes=[
                pltpu.VMEM((size, kinds, rows * tiles, LANES), f32),
                pltpu.SemaphoreType.DMA((size,)),
            ]
            + [pltpu.VMEM((STEPS, rows + 2 * DEEP, tiles, LANES), f32)] * 3,
            input_output_aliases={5: 0} if out else {},
            compiler_params=PARAMS,
            name="steps",
        )(order, *parts, coef, *out)

    def rest(late, pieces, coef, table, order, gone, base):
        chosen = pl.pallas_call(
            functools.partial(pick_kernel, members),
            in_specs=[SM, VM],
            out_specs=VM,
            out_shape=jax.ShapeDtypeStruct((blocks, late, kinds * rows, LANES), f32),
            compiler_params=PARAMS,
            name="pick",
        )(table, pieces)
        routed = lax.all_to_all(chosen, "dom", 0, 0, tiled=True).reshape(-1, LANES)
        routed, base = lax.optimization_barrier((routed, base))
        low = 0
        chunks = []
        for size in CHUNKS:
            chunks.append((low, size, prepared(low, size, gone, base, routed)))
            low += size
        out = []
        for low, size, parts in chunks:
            out = [stepped(low, size, order, parts, coef, out)]
        return out[0]

    args = lax.optimization_barrier((pieces, coef, table, order, gone, base))
    which = jnp.clip(most - SIZES[0], 0, len(SIZES) - 1)
    out = lax.switch(which, [functools.partial(rest, size) for size in SIZES], *args)
    out = out.reshape(members, kinds, bands, tiles, SUB, LANES)
    return jnp.swapaxes(out, -3, -2).reshape(state.shape)


def solution(mesh):
    placed = (
        P(),
        P("dom", None, "space", None),
        P("dom", None, "space", None),
        P("space", None),
        P("space", None),
        P("space", None),
    )
    return jax.shard_map(
        local, mesh=mesh, in_specs=placed, out_specs=P("dom", None, "space", None), check_vma=False
    )
```

```python
import functools

import jax
import jax.numpy as jnp
from jax import lax
from jax.experimental import pallas as pl
from jax.experimental.pallas import tpu as pltpu
from jax.sharding import PartitionSpec as P

STEPS = 4
CAP = 2
DT = 0.3
LANES = 128
SUB = 8
DEEP = 8
RIM = (7, 7, 8)
RIMS = sum(RIM)
FROM = (0, 7, 14)
CHUNKS = (2, 2)
SIZES = (2, 3, 4)

VM = pl.BlockSpec(memory_space=pltpu.VMEM)
SM = pl.BlockSpec(memory_space=pltpu.SMEM)
HB = pl.BlockSpec(memory_space=pltpu.HBM)
PARAMS = pltpu.CompilerParams(vmem_limit_bytes=24 << 20)


def pack_kernel(members, anc, state, out, held, sem):
    fetched = [pltpu.make_async_copy(state.at[k], held.at[k], sem.at[0, k]) for k in range(members)]
    for c in fetched:
        c.start()
    me = lax.axis_index("dom")
    bits = jnp.int32(0)
    for j in range(anc.shape[0]):
        a = anc[j]
        hit = (a != j) & (a // members == me)
        bits = bits | jnp.where(hit, jnp.left_shift(1, a % members), 0)
    first = jnp.int32(members - 1)
    for k in reversed(range(members)):
        first = jnp.where((bits >> k) & 1 == 1, k, first)
    second = jnp.int32(members - 1)
    for k in reversed(range(members)):
        second = jnp.where(((bits >> k) & 1 == 1) & (k != first), k, second)
    for c in fetched:
        c.wait()
    copies = []
    for q, p in enumerate((first, second)):
        for f in range(state.shape[1]):
            for t in range(state.shape[2]):
                copies.append(
                    pltpu.make_async_copy(held.at[p, f, t], out.at[:, q, f, t], sem.at[1, len(copies)])
                )
    for c in copies:
        c.start()
    for c in copies:
        c.wait()


def plan_kernel(members, anc, table, order, gone, most, donors):
    slots = anc.shape[0]
    for b in range(slots // members):
        donors[b] = 0
    for j in range(slots):
        a = anc[j]
        donors[a // members] |= jnp.where(a != j, jnp.left_shift(1, a % members), 0)
    worst = jnp.int32(0)
    for b in range(slots // members):
        moved = [jnp.where(anc[b * members + k] != b * members + k, 1, 0) for k in range(members)]
        stay = members - sum(moved)
        worst = jnp.maximum(worst, members - stay)
        ahead = jnp.int32(0)
        for k in range(members):
            a = anc[b * members + k]
            below = donors[a // members] & (jnp.left_shift(1, a % members) - 1)
            turn = jnp.where(moved[k] == 1, stay + ahead, k - ahead)
            table[b * members + turn] = a // members * CAP + jnp.where(below != 0, 1, 0)
            ahead += moved[k]
    most[0] = worst
    at = lax.axis_index("dom") * members
    moved = [jnp.where(anc[at + k] != at + k, 1, 0) for k in range(members)]
    stay = members - sum(moved)
    ahead = jnp.int32(0)
    for k in range(members):
        turn = jnp.where(moved[k] == 1, stay + ahead, k - ahead)
        order[turn] = k
        gone[turn] = moved[k]
        ahead += moved[k]


def rim_kernel(depth, coriolis, drag, first, second, sem):
    toward = 1 - lax.axis_index("space") % 2
    last = depth.shape[0] - 1
    copies = []
    for n, ref in enumerate((depth, coriolis, drag)):
        for out, at in ((first, toward * last), (second, (1 - toward) * last)):
            copies.append(pltpu.make_async_copy(ref.at[at], out.at[n], sem.at[len(copies)]))
    for c in copies:
        c.start()
    for c in copies:
        c.wait()


def coef_kernel(depth, coriolis, drag, first, second, out):
    tiles = out.shape[2]
    bands = depth.shape[0] // (tiles * SUB)
    odd = lax.axis_index("space") % 2 == 1
    for r in range(out.shape[1]):
        band, row = r // SUB - 1, r % SUB
        values = []
        for n, own in enumerate((depth, coriolis, drag)):
            if 0 <= band < bands:
                values.append(own[pl.ds(band * tiles * SUB + row, tiles, stride=SUB), :])
            else:
                at = pl.ds(n * tiles * SUB + row, tiles, stride=SUB)
                values.append(jnp.where(odd == (band < 0), first[at, :], second[at, :]))
        out[0, r] = (0.5 * DT) * values[0]
        out[1, r] = DT * values[1]
        out[2, r] = 1.0 / (1.0 + DT * values[2])


def pick_kernel(members, table, got, out):
    size = out.shape[1]
    for d in range(out.shape[0]):
        for k in range(size):
            out[d, k] = got[table[(d + 1) * members - size + k]]


def base_kernel(order, gone, state, jitter, out):
    members, kinds, rows, tiles = out.shape[:4]
    for k in range(members):
        slot = order[k]
        mine = gone[k] == 0
        for f in range(kinds):
            for r in range(rows):
                near = pl.ds((f * (rows // SUB) + r // SUB) * tiles * SUB + r % SUB, tiles, stride=SUB)
                out[k, f, r] = jnp.where(mine, state[slot, near, :], 0.0) + jitter[slot, near, :]


def prep_kernel(low, gone, base, routed, fields, first, second):
    size, kinds, rows, tiles = fields.shape[:4]
    slab = kinds * rows
    late = routed.shape[0] // (tiles * slab)
    odd = lax.axis_index("space") % 2 == 1
    for k in range(size):
        at = low + k - (base.shape[0] - late)
        mine = gone[low + k] == 0
        for f in range(kinds):
            values = []
            for r in range(rows):
                value = base[low + k, f, r]
                if at >= 0:
                    far = routed[pl.ds(at * slab + f * rows + r, tiles, stride=late * slab), :]
                    value = jnp.where(mine, value, value + far)
                fields[k, f, r] = value
                values.append(value)
            for r in range(RIM[f]):
                top, bottom = values[r], values[rows - RIM[f] + r]
                first[k, FROM[f] + r] = jnp.where(odd, top, bottom)
                second[k, FROM[f] + r] = jnp.where(odd, bottom, top)


def step_kernel(low, order, fields, first, second, coef, *rest):
    whole, out, sem, *held = rest[-6:]
    size, kinds, rows, tiles = fields.shape[:4]
    lane = lax.broadcasted_iota(jnp.int32, (tiles, LANES), 1)
    tile = lax.broadcasted_iota(jnp.int32, (tiles, LANES), 0)
    lane_first, lane_last = lane == 0, lane == LANES - 1
    wall_first = lane_first & (tile == 0)
    wall_last = lane_last & (tile == tiles - 1)
    half = 0.5 * DT
    odd = lax.axis_index("space") % 2 == 1

    def difference(x, edge):
        before = pltpu.roll(jnp.where(lane_last, pltpu.roll(x, 1, 0), x), 1, 1)
        after = pltpu.roll(jnp.where(lane_first, pltpu.roll(x, tiles - 1, 0), x), LANES - 1, 1)
        return jnp.where(wall_last, edge, after) - jnp.where(wall_first, edge, before)

    def const(n, r):
        return coef[n, r + DEEP]

    def particle(k, carry):
        def get(n, f, r):
            if n:
                return held[f][n - 1, r + DEEP]
            if 0 <= r < rows:
                return fields[k, f, r]
            at = FROM[f] + (r + RIM[f] if r < 0 else r - rows)
            return jnp.where(odd == (r < 0), first[k, at], second[k, at])

        def put(n, f, r, value):
            if n < STEPS or f == 0:
                held[f][n - 1, r + DEEP] = value
            if n == STEPS and 0 <= r < rows:
                at = pl.ds(r // SUB * tiles * SUB + r % SUB, tiles, stride=SUB)
                out[k, f, at, :] = value

        for n in range(STEPS):
            left = STEPS - 1 - n
            low_u, high_u = (1 - 2 * left, rows + 2 * left - 1) if left else (0, rows)
            for r in range(-(2 * left + 1), rows + 2 * left + 1):
                across = difference(const(0, r) * get(n, 1, r), 0.0)
                along = const(0, r + 1) * get(n, 2, r + 1) - const(0, r - 1) * get(n, 2, r - 1)
                put(n + 1, 0, r, get(n, 0, r) - (across + along))
            for r in range(-2 * left, rows + 2 * left):
                uu, vv, c, s = get(n, 1, r), get(n, 2, r), const(1, r), const(2, r)
                if low_u <= r < high_u:
                    here = get(n + 1, 0, r)
                    put(n + 1, 1, r, s * (uu + c * vv - half * difference(here, here)))
                along = get(n + 1, 0, r + 1) - get(n + 1, 0, r - 1)
                put(n + 1, 2, r, s * (vv - c * uu - half * along))
        copy_out(k).start()
        return carry

    def copy_out(k):
        return pltpu.make_async_copy(out.at[k], whole.at[order[low + k]], sem.at[k])

    lax.fori_loop(0, size, particle, 0)
    for k in range(size):
        copy_out(k).wait()


def local(ancestor, state, jitter, depth, coriolis, drag):
    members, kinds, rows, width = state.shape
    tiles, bands = width // LANES, rows // SUB
    blocks = lax.axis_size("dom")
    count = lax.axis_size("space")
    swap_first = [(i, i ^ 1) for i in range(count)]
    swap_second = [(i, (i + 2 * (i % 2) - 1) % count) for i in range(count)]
    f32 = jnp.float32

    def tiled(x):
        x = x.reshape(x.shape[:-2] + (x.shape[-2] // SUB, SUB, tiles, LANES))
        return jnp.swapaxes(x, -3, -2)

    state_t, jitter_t = tiled(state), tiled(jitter)

    packed = pl.pallas_call(
        functools.partial(pack_kernel, members),
        in_specs=[SM, HB],
        out_specs=HB,
        out_shape=jax.ShapeDtypeStruct((tiles, CAP, kinds, bands, SUB, LANES), f32),
        scratch_shapes=[
            pltpu.VMEM((members, kinds, bands, tiles, SUB, LANES), f32),
            pltpu.SemaphoreType.DMA((2, CAP * kinds * bands)),
        ],
        compiler_params=PARAMS,
        name="pack",
    )(ancestor, pltpu.with_memory_space_constraint(state_t, pltpu.HBM))
    table, order, gone, most = pl.pallas_call(
        functools.partial(plan_kernel, members),
        in_specs=[SM],
        out_specs=(SM, SM, SM, SM),
        out_shape=[
            jax.ShapeDtypeStruct((n,), jnp.int32) for n in (ancestor.shape[0], members, members, 1)
        ],
        scratch_shapes=[pltpu.SMEM((blocks,), jnp.int32)],
        compiler_params=PARAMS,
        name="plan",
    )(ancestor)

    packed, *raw = lax.optimization_barrier((packed, depth, coriolis, drag))
    pieces = lax.all_to_all(packed, "dom", 0, 0, tiled=True)
    pieces = pieces.reshape(blocks * CAP, kinds * rows, LANES)
    rim = jax.ShapeDtypeStruct((3, tiles, SUB, LANES), f32)
    rims = pl.pallas_call(
        rim_kernel,
        in_specs=[HB] * 3,
        out_specs=(VM, VM),
        out_shape=(rim, rim),
        scratch_shapes=[pltpu.SemaphoreType.DMA((6,))],
        compiler_params=PARAMS,
        name="rims",
    )(*(pltpu.with_memory_space_constraint(tiled(x), pltpu.HBM) for x in raw))
    rims = (lax.ppermute(rims[0], "space", swap_first), lax.ppermute(rims[1], "space", swap_second))
    coef = pl.pallas_call(
        coef_kernel,
        in_specs=[VM] * 5,
        out_specs=VM,
        out_shape=jax.ShapeDtypeStruct((3, rows + 2 * DEEP, tiles, LANES), f32),
        compiler_params=PARAMS,
        name="coef",
    )(
        *(tiled(x).reshape(rows * tiles, LANES) for x in raw),
        *(x.reshape(3 * tiles * SUB, LANES) for x in rims),
    )
    sides = (members, kinds * rows * tiles, LANES)
    state_t, jitter_t = state_t.reshape(sides), jitter_t.reshape(sides)

    base = pl.pallas_call(
        base_kernel,
        in_specs=[SM, SM, VM, VM],
        out_specs=VM,
        out_shape=jax.ShapeDtypeStruct((members, kinds, rows, tiles, LANES), f32),
        compiler_params=PARAMS,
        name="base",
    )(order, gone, state_t, jitter_t)

    def prepared(low, size, gone, base, routed):
        rim = jax.ShapeDtypeStruct((size, RIMS, tiles, LANES), f32)
        fields, first, second = pl.pallas_call(
            functools.partial(prep_kernel, low),
            in_specs=[SM, VM, VM],
            out_specs=(VM, VM, VM),
            out_shape=(jax.ShapeDtypeStruct((size, kinds, rows, tiles, LANES), f32), rim, rim),
            compiler_params=PARAMS,
            name="prep",
        )(gone, base, routed)
        first = lax.ppermute(first, "space", swap_first)
        second = lax.ppermute(second, "space", swap_second)
        return fields, first, second

    def stepped(low, size, order, parts, coef, out):
        return pl.pallas_call(
            functools.partial(step_kernel, low),
            in_specs=[SM] + [VM] * 4 + [HB] * len(out),
            out_specs=HB,
            out_shape=jax.ShapeDtypeStruct((members, kinds, rows * tiles, LANES), f32),
            scratch_shapes=[
                pltpu.VMEM((size, kinds, rows * tiles, LANES), f32),
                pltpu.SemaphoreType.DMA((size,)),
            ]
            + [pltpu.VMEM((STEPS, rows + 2 * DEEP, tiles, LANES), f32)] * 3,
            input_output_aliases={5: 0} if out else {},
            compiler_params=PARAMS,
            name="steps",
        )(order, *parts, coef, *out)

    def rest(late, pieces, coef, table, order, gone, base):
        chosen = pl.pallas_call(
            functools.partial(pick_kernel, members),
            in_specs=[SM, VM],
            out_specs=VM,
            out_shape=jax.ShapeDtypeStruct((blocks, late, kinds * rows, LANES), f32),
            compiler_params=PARAMS,
            name="pick",
        )(table, pieces)
        routed = lax.all_to_all(chosen, "dom", 0, 0, tiled=True).reshape(-1, LANES)
        routed, base = lax.optimization_barrier((routed, base))
        low = 0
        chunks = []
        for size in CHUNKS:
            chunks.append((low, size, prepared(low, size, gone, base, routed)))
            low += size
        out = []
        for low, size, parts in chunks:
            out = [stepped(low, size, order, parts, coef, out)]
        return out[0]

    args = lax.optimization_barrier((pieces, coef, table, order, gone, base))
    which = jnp.clip(most[0] - SIZES[0], 0, len(SIZES) - 1)
    out = lax.switch(which, [functools.partial(rest, size) for size in SIZES], *args)
    out = out.reshape(members, kinds, bands, tiles, SUB, LANES)
    return jnp.swapaxes(out, -3, -2).reshape(state.shape)


def solution(mesh):
    placed = (
        P(),
        P("dom", None, "space", None),
        P("dom", None, "space", None),
        P("space", None),
        P("space", None),
        P("space", None),
    )
    return jax.shard_map(
        local, mesh=mesh, in_specs=placed, out_specs=P("dom", None, "space", None), check_vma=False
    )
```

```python
import functools

import jax
import jax.numpy as jnp
from jax import lax
from jax.experimental import pallas as pl
from jax.experimental.pallas import tpu as pltpu
from jax.sharding import PartitionSpec as P

STEPS = 4
CAP = 2
DT = 0.3
LANES = 128
SUB = 8
DEEP = 8
RIM = (7, 7, 8)
RIMS = sum(RIM)
FROM = (0, 7, 14)
CHUNKS = (3, 1)
SIZES = (2, 3, 4)

VM = pl.BlockSpec(memory_space=pltpu.VMEM)
SM = pl.BlockSpec(memory_space=pltpu.SMEM)
HB = pl.BlockSpec(memory_space=pltpu.HBM)
PARAMS = pltpu.CompilerParams(vmem_limit_bytes=24 << 20)


def pack_kernel(members, ancestor, state, out, anc, held, sem):
    known = pltpu.make_async_copy(ancestor, anc, sem.at[0, members])
    known.start()
    fetched = [pltpu.make_async_copy(state.at[k], held.at[k], sem.at[0, k]) for k in range(members)]
    for c in fetched:
        c.start()
    known.wait()
    me = lax.axis_index("dom")
    bits = jnp.int32(0)
    for j in range(anc.shape[0]):
        a = anc[j]
        hit = (a != j) & (a // members == me)
        bits = bits | jnp.where(hit, jnp.left_shift(1, a % members), 0)
    first = jnp.int32(members - 1)
    for k in reversed(range(members)):
        first = jnp.where((bits >> k) & 1 == 1, k, first)
    second = jnp.int32(members - 1)
    for k in reversed(range(members)):
        second = jnp.where(((bits >> k) & 1 == 1) & (k != first), k, second)
    for c in fetched:
        c.wait()
    copies = []
    for q, p in enumerate((first, second)):
        for f in range(state.shape[1]):
            for t in range(state.shape[2]):
                copies.append(
                    pltpu.make_async_copy(held.at[p, f, t], out.at[:, q, f, t], sem.at[1, len(copies)])
                )
    for c in copies:
        c.start()
    for c in copies:
        c.wait()


def plan_kernel(members, anc, table, order, gone, most, donors):
    slots = anc.shape[0]
    for b in range(slots // members):
        donors[b] = 0
    for j in range(slots):
        a = anc[j]
        donors[a // members] |= jnp.where(a != j, jnp.left_shift(1, a % members), 0)
    worst = jnp.int32(0)
    for b in range(slots // members):
        moved = [jnp.where(anc[b * members + k] != b * members + k, 1, 0) for k in range(members)]
        stay = members - sum(moved)
        worst = jnp.maximum(worst, members - stay)
        ahead = jnp.int32(0)
        for k in range(members):
            a = anc[b * members + k]
            below = donors[a // members] & (jnp.left_shift(1, a % members) - 1)
            turn = jnp.where(moved[k] == 1, stay + ahead, k - ahead)
            table[b * members + turn] = a // members * CAP + jnp.where(below != 0, 1, 0)
            ahead += moved[k]
    most[0] = worst
    at = lax.axis_index("dom") * members
    moved = [jnp.where(anc[at + k] != at + k, 1, 0) for k in range(members)]
    stay = members - sum(moved)
    ahead = jnp.int32(0)
    for k in range(members):
        turn = jnp.where(moved[k] == 1, stay + ahead, k - ahead)
        order[turn] = k
        gone[turn] = moved[k]
        ahead += moved[k]


def rim_kernel(depth, coriolis, drag, first, second, sem):
    toward = 1 - lax.axis_index("space") % 2
    last = depth.shape[0] - 1
    part = first.shape[1]
    mine = pl.ds(lax.axis_index("dom") % 2 * part, part)
    copies = []
    for n, ref in enumerate((depth, coriolis, drag)):
        for out, at in ((first, toward * last), (second, (1 - toward) * last)):
            copies.append(pltpu.make_async_copy(ref.at[at, mine], out.at[n], sem.at[len(copies)]))
    for c in copies:
        c.start()
    for c in copies:
        c.wait()


def coef_kernel(depth, coriolis, drag, first, second, first_other, second_other, out):
    tiles = out.shape[2]
    part = tiles // 2
    bands = depth.shape[0] // (tiles * SUB)
    odd = lax.axis_index("space") % 2 == 1
    high = lax.axis_index("dom") % 2 == 1
    for r in range(out.shape[1]):
        band, row = r // SUB - 1, r % SUB
        values = []
        for n, own in enumerate((depth, coriolis, drag)):
            if 0 <= band < bands:
                values.append(own[pl.ds(band * tiles * SUB + row, tiles, stride=SUB), :])
            else:
                at = pl.ds(n * part * SUB + row, part, stride=SUB)
                ahead = odd == (band < 0)
                mine = jnp.where(ahead, first[at, :], second[at, :])
                other = jnp.where(ahead, first_other[at, :], second_other[at, :])
                halves = jnp.where(high, other, mine), jnp.where(high, mine, other)
                values.append(jnp.concatenate(halves, axis=0))
        out[0, r] = (0.5 * DT) * values[0]
        out[1, r] = DT * values[1]
        out[2, r] = 1.0 / (1.0 + DT * values[2])


def pick_kernel(members, table, got, out):
    size = out.shape[1]
    for d in range(out.shape[0]):
        for k in range(size):
            out[d, k] = got[table[(d + 1) * members - size + k]]


def base_kernel(order, gone, state, jitter, out):
    members, kinds, rows, tiles = out.shape[:4]
    for k in range(members):
        slot = order[k]
        mine = gone[k] == 0
        for f in range(kinds):
            for r in range(rows):
                near = pl.ds((f * (rows // SUB) + r // SUB) * tiles * SUB + r % SUB, tiles, stride=SUB)
                out[k, f, r] = jnp.where(mine, state[slot, near, :], 0.0) + jitter[slot, near, :]


def prep_kernel(low, gone, base, routed, fields, first, second):
    size, kinds, rows, tiles = fields.shape[:4]
    slab = kinds * rows
    late = routed.shape[0] // (tiles * slab)
    odd = lax.axis_index("space") % 2 == 1
    for k in range(size):
        at = low + k - (base.shape[0] - late)
        mine = gone[low + k] == 0
        for f in range(kinds):
            values = []
            for r in range(rows):
                value = base[low + k, f, r]
                if at >= 0:
                    far = routed[pl.ds(at * slab + f * rows + r, tiles, stride=late * slab), :]
                    value = jnp.where(mine, value, value + far)
                fields[k, f, r] = value
                values.append(value)
            for r in range(RIM[f]):
                top, bottom = values[r], values[rows - RIM[f] + r]
                first[k, FROM[f] + r] = jnp.where(odd, top, bottom)
                second[k, FROM[f] + r] = jnp.where(odd, bottom, top)


def step_kernel(low, order, fields, first, second, coef, *rest):
    whole, out, sem, *held = rest[-6:]
    size, kinds, rows, tiles = fields.shape[:4]
    lane = lax.broadcasted_iota(jnp.int32, (tiles, LANES), 1)
    tile = lax.broadcasted_iota(jnp.int32, (tiles, LANES), 0)
    lane_first, lane_last = lane == 0, lane == LANES - 1
    wall_first = lane_first & (tile == 0)
    wall_last = lane_last & (tile == tiles - 1)
    half = 0.5 * DT
    odd = lax.axis_index("space") % 2 == 1

    def difference(x, edge):
        before = pltpu.roll(jnp.where(lane_last, pltpu.roll(x, 1, 0), x), 1, 1)
        after = pltpu.roll(jnp.where(lane_first, pltpu.roll(x, tiles - 1, 0), x), LANES - 1, 1)
        return jnp.where(wall_last, edge, after) - jnp.where(wall_first, edge, before)

    def const(n, r):
        return coef[n, r + DEEP]

    def particle(k, carry):
        def get(n, f, r):
            if n:
                return held[f][n - 1, r + DEEP]
            if 0 <= r < rows:
                return fields[k, f, r]
            at = FROM[f] + (r + RIM[f] if r < 0 else r - rows)
            return jnp.where(odd == (r < 0), first[k, at], second[k, at])

        def put(n, f, r, value):
            if n < STEPS or f == 0:
                held[f][n - 1, r + DEEP] = value
            if n == STEPS and 0 <= r < rows:
                at = pl.ds(r // SUB * tiles * SUB + r % SUB, tiles, stride=SUB)
                out[k, f, at, :] = value

        for n in range(STEPS):
            left = STEPS - 1 - n
            low_u, high_u = (1 - 2 * left, rows + 2 * left - 1) if left else (0, rows)
            for r in range(-(2 * left + 1), rows + 2 * left + 1):
                across = difference(const(0, r) * get(n, 1, r), 0.0)
                along = const(0, r + 1) * get(n, 2, r + 1) - const(0, r - 1) * get(n, 2, r - 1)
                put(n + 1, 0, r, get(n, 0, r) - (across + along))
            for r in range(-2 * left, rows + 2 * left):
                uu, vv, c, s = get(n, 1, r), get(n, 2, r), const(1, r), const(2, r)
                if low_u <= r < high_u:
                    here = get(n + 1, 0, r)
                    put(n + 1, 1, r, s * (uu + c * vv - half * difference(here, here)))
                along = get(n + 1, 0, r + 1) - get(n + 1, 0, r - 1)
                put(n + 1, 2, r, s * (vv - c * uu - half * along))
        copy_out(k).start()
        return carry

    def copy_out(k):
        return pltpu.make_async_copy(out.at[k], whole.at[order[low + k]], sem.at[k])

    lax.fori_loop(0, size, particle, 0)
    for k in range(size):
        copy_out(k).wait()


def local(ancestor, state, jitter, depth, coriolis, drag):
    members, kinds, rows, width = state.shape
    tiles, bands = width // LANES, rows // SUB
    blocks = lax.axis_size("dom")
    count = lax.axis_size("space")
    swap_first = [(i, i ^ 1) for i in range(count)]
    swap_second = [(i, (i + 2 * (i % 2) - 1) % count) for i in range(count)]
    f32 = jnp.float32

    def tiled(x):
        x = x.reshape(x.shape[:-2] + (x.shape[-2] // SUB, SUB, tiles, LANES))
        return jnp.swapaxes(x, -3, -2)

    state_t, jitter_t = tiled(state), tiled(jitter)

    packed = pl.pallas_call(
        functools.partial(pack_kernel, members),
        in_specs=[HB, HB],
        out_specs=HB,
        out_shape=jax.ShapeDtypeStruct((tiles, CAP, kinds, bands, SUB, LANES), f32),
        scratch_shapes=[
            pltpu.SMEM(ancestor.shape, jnp.int32),
            pltpu.VMEM((members, kinds, bands, tiles, SUB, LANES), f32),
            pltpu.SemaphoreType.DMA((2, CAP * kinds * bands)),
        ],
        compiler_params=PARAMS,
        name="pack",
    )(*(pltpu.with_memory_space_constraint(x, pltpu.HBM) for x in (ancestor, state_t)))
    table, order, gone, most = pl.pallas_call(
        functools.partial(plan_kernel, members),
        in_specs=[SM],
        out_specs=(SM, SM, SM, SM),
        out_shape=[
            jax.ShapeDtypeStruct((n,), jnp.int32) for n in (ancestor.shape[0], members, members, 1)
        ],
        scratch_shapes=[pltpu.SMEM((blocks,), jnp.int32)],
        compiler_params=PARAMS,
        name="plan",
    )(ancestor)

    sides = (members, kinds * rows * tiles, LANES)
    state_t, jitter_t = state_t.reshape(sides), jitter_t.reshape(sides)

    base = pl.pallas_call(
        base_kernel,
        in_specs=[SM, SM, VM, VM],
        out_specs=VM,
        out_shape=jax.ShapeDtypeStruct((members, kinds, rows, tiles, LANES), f32),
        compiler_params=PARAMS,
        name="base",
    )(order, gone, state_t, jitter_t)

    packed, *raw = lax.optimization_barrier((packed, depth, coriolis, drag))
    pieces = lax.all_to_all(packed, "dom", 0, 0, tiled=True)
    pieces = pieces.reshape(blocks * CAP, kinds * rows, LANES)
    rim = jax.ShapeDtypeStruct((3, tiles // 2, SUB, LANES), f32)
    rims = pl.pallas_call(
        rim_kernel,
        in_specs=[HB] * 3,
        out_specs=(VM, VM),
        out_shape=(rim, rim),
        scratch_shapes=[pltpu.SemaphoreType.DMA((6,))],
        compiler_params=PARAMS,
        name="rims",
    )(*(pltpu.with_memory_space_constraint(tiled(x), pltpu.HBM) for x in raw))
    rims = [lax.ppermute(rims[0], "space", swap_first), lax.ppermute(rims[1], "space", swap_second)]
    *rims, table, order, gone, base = lax.optimization_barrier((*rims, table, order, gone, base))
    rims += [lax.ppermute(x, "dom", [(i, i ^ 1) for i in range(blocks)]) for x in rims]
    coef = pl.pallas_call(
        coef_kernel,
        in_specs=[VM] * 7,
        out_specs=VM,
        out_shape=jax.ShapeDtypeStruct((3, rows + 2 * DEEP, tiles, LANES), f32),
        compiler_params=PARAMS,
        name="coef",
    )(
        *(tiled(x).reshape(rows * tiles, LANES) for x in raw),
        *(x.reshape(-1, LANES) for x in rims),
    )
    def prepared(low, size, gone, base, routed):
        rim = jax.ShapeDtypeStruct((size, RIMS, tiles, LANES), f32)
        fields, first, second = pl.pallas_call(
            functools.partial(prep_kernel, low),
            in_specs=[SM, VM, VM],
            out_specs=(VM, VM, VM),
            out_shape=(jax.ShapeDtypeStruct((size, kinds, rows, tiles, LANES), f32), rim, rim),
            compiler_params=PARAMS,
            name="prep",
        )(gone, base, routed)
        first = lax.ppermute(first, "space", swap_first)
        second = lax.ppermute(second, "space", swap_second)
        return fields, first, second

    def stepped(low, size, order, parts, coef, out):
        return pl.pallas_call(
            functools.partial(step_kernel, low),
            in_specs=[SM] + [VM] * 4 + [HB] * len(out),
            out_specs=HB,
            out_shape=jax.ShapeDtypeStruct((members, kinds, rows * tiles, LANES), f32),
            scratch_shapes=[
                pltpu.VMEM((size, kinds, rows * tiles, LANES), f32),
                pltpu.SemaphoreType.DMA((size,)),
            ]
            + [pltpu.VMEM((STEPS, rows + 2 * DEEP, tiles, LANES), f32)] * 3,
            input_output_aliases={5: 0} if out else {},
            compiler_params=PARAMS,
            name="steps",
        )(order, *parts, coef, *out)

    def rest(late, pieces, coef, table, order, gone, base):
        chosen = pl.pallas_call(
            functools.partial(pick_kernel, members),
            in_specs=[SM, VM],
            out_specs=VM,
            out_shape=jax.ShapeDtypeStruct((blocks, late, kinds * rows, LANES), f32),
            compiler_params=PARAMS,
            name="pick",
        )(table, pieces)
        routed = lax.all_to_all(chosen, "dom", 0, 0, tiled=True).reshape(-1, LANES)
        routed, base = lax.optimization_barrier((routed, base))
        low = 0
        chunks = []
        for size in CHUNKS:
            chunks.append((low, size, prepared(low, size, gone, base, routed)))
            low += size
        out = []
        for low, size, parts in chunks:
            out = [stepped(low, size, order, parts, coef, out)]
        return out[0]

    args = lax.optimization_barrier((pieces, coef, table, order, gone, base))
    which = jnp.clip(most[0] - SIZES[0], 0, len(SIZES) - 1)
    out = lax.switch(which, [functools.partial(rest, size) for size in SIZES], *args)
    out = out.reshape(members, kinds, bands, tiles, SUB, LANES)
    return jnp.swapaxes(out, -3, -2).reshape(state.shape)


def solution(mesh):
    placed = (
        P(),
        P("dom", None, "space", None),
        P("dom", None, "space", None),
        P("space", None),
        P("space", None),
        P("space", None),
    )
    return jax.shard_map(
        local, mesh=mesh, in_specs=placed, out_specs=P("dom", None, "space", None), check_vma=False
    )
```

```python
import functools

import jax
import jax.numpy as jnp
from jax import lax
from jax.experimental import pallas as pl
from jax.experimental.pallas import tpu as pltpu
from jax.sharding import PartitionSpec as P

STEPS = 4
CAP = 2
DT = 0.3
LANES = 128
SUB = 8
DEEP = 8
RIM = (7, 7, 8)
RIMS = sum(RIM)
FROM = (0, 7, 14)
CHUNKS = (2, 2)
SIZES = (2, 3, 4)

VM = pl.BlockSpec(memory_space=pltpu.VMEM)
SM = pl.BlockSpec(memory_space=pltpu.SMEM)
HB = pl.BlockSpec(memory_space=pltpu.HBM)
PARAMS = pltpu.CompilerParams(vmem_limit_bytes=24 << 20)


def pack_kernel(members, ancestor, state, out, anc, held, sem):
    known = pltpu.make_async_copy(ancestor, anc, sem.at[0, members])
    known.start()
    fetched = [pltpu.make_async_copy(state.at[k], held.at[k], sem.at[0, k]) for k in range(members)]
    for c in fetched:
        c.start()
    known.wait()
    me = lax.axis_index("dom")
    bits = jnp.int32(0)
    for j in range(anc.shape[0]):
        a = anc[j]
        hit = (a != j) & (a // members == me)
        bits = bits | jnp.where(hit, jnp.left_shift(1, a % members), 0)
    first = jnp.int32(members - 1)
    for k in reversed(range(members)):
        first = jnp.where((bits >> k) & 1 == 1, k, first)
    second = jnp.int32(members - 1)
    for k in reversed(range(members)):
        second = jnp.where(((bits >> k) & 1 == 1) & (k != first), k, second)
    for c in fetched:
        c.wait()
    copies = []
    for q, p in enumerate((first, second)):
        for f in range(state.shape[1]):
            for t in range(state.shape[2]):
                copies.append(
                    pltpu.make_async_copy(held.at[p, f, t], out.at[:, q, f, t], sem.at[1, len(copies)])
                )
    for c in copies:
        c.start()
    for c in copies:
        c.wait()


def plan_kernel(members, anc, table, order, gone, most, donors):
    slots = anc.shape[0]
    for b in range(slots // members):
        donors[b] = 0
    for j in range(slots):
        a = anc[j]
        donors[a // members] |= jnp.where(a != j, jnp.left_shift(1, a % members), 0)
    worst = jnp.int32(0)
    for b in range(slots // members):
        moved = [jnp.where(anc[b * members + k] != b * members + k, 1, 0) for k in range(members)]
        stay = members - sum(moved)
        worst = jnp.maximum(worst, members - stay)
        ahead = jnp.int32(0)
        for k in range(members):
            a = anc[b * members + k]
            below = donors[a // members] & (jnp.left_shift(1, a % members) - 1)
            turn = jnp.where(moved[k] == 1, stay + ahead, k - ahead)
            table[b * members + turn] = a // members * CAP + jnp.where(below != 0, 1, 0)
            ahead += moved[k]
    most[0] = worst
    at = lax.axis_index("dom") * members
    moved = [jnp.where(anc[at + k] != at + k, 1, 0) for k in range(members)]
    stay = members - sum(moved)
    ahead = jnp.int32(0)
    for k in range(members):
        turn = jnp.where(moved[k] == 1, stay + ahead, k - ahead)
        order[turn] = k
        gone[turn] = moved[k]
        ahead += moved[k]


def rim_kernel(depth, coriolis, drag, first, second, sem):
    toward = 1 - lax.axis_index("space") % 2
    last = depth.shape[0] - 1
    part = first.shape[1]
    mine = pl.ds(lax.axis_index("dom") % 2 * part, part)
    copies = []
    for n, ref in enumerate((depth, coriolis, drag)):
        for out, at in ((first, toward * last), (second, (1 - toward) * last)):
            copies.append(pltpu.make_async_copy(ref.at[at, mine], out.at[n], sem.at[len(copies)]))
    for c in copies:
        c.start()
    for c in copies:
        c.wait()


def coef_kernel(depth, coriolis, drag, first, second, first_other, second_other, out):
    tiles = out.shape[2]
    part = tiles // 2
    bands = depth.shape[0] // (tiles * SUB)
    odd = lax.axis_index("space") % 2 == 1
    high = lax.axis_index("dom") % 2 == 1
    for r in range(out.shape[1]):
        band, row = r // SUB - 1, r % SUB
        values = []
        for n, own in enumerate((depth, coriolis, drag)):
            if 0 <= band < bands:
                values.append(own[pl.ds(band * tiles * SUB + row, tiles, stride=SUB), :])
            else:
                at = pl.ds(n * part * SUB + row, part, stride=SUB)
                ahead = odd == (band < 0)
                mine = jnp.where(ahead, first[at, :], second[at, :])
                other = jnp.where(ahead, first_other[at, :], second_other[at, :])
                halves = jnp.where(high, other, mine), jnp.where(high, mine, other)
                values.append(jnp.concatenate(halves, axis=0))
        out[0, r] = (0.5 * DT) * values[0]
        out[1, r] = DT * values[1]
        out[2, r] = 1.0 / (1.0 + DT * values[2])


def pick_kernel(members, table, got, out):
    size = out.shape[1]
    for d in range(out.shape[0]):
        for k in range(size):
            out[d, k] = got[table[(d + 1) * members - size + k]]


def base_kernel(order, gone, state, jitter, out):
    members, kinds, rows, tiles = out.shape[:4]
    for k in range(members):
        slot = order[k]
        mine = gone[k] == 0
        for f in range(kinds):
            for r in range(rows):
                near = pl.ds((f * (rows // SUB) + r // SUB) * tiles * SUB + r % SUB, tiles, stride=SUB)
                out[k, f, r] = jnp.where(mine, state[slot, near, :], 0.0) + jitter[slot, near, :]


def prep_kernel(low, gone, base, routed, fields, first, second):
    size, kinds, rows, tiles = fields.shape[:4]
    slab = kinds * rows
    late = routed.shape[0] // (tiles * slab)
    odd = lax.axis_index("space") % 2 == 1
    for k in range(size):
        at = low + k - (base.shape[0] - late)
        mine = gone[low + k] == 0
        for f in range(kinds):
            values = []
            for r in range(rows):
                value = base[low + k, f, r]
                if at >= 0:
                    far = routed[pl.ds(at * slab + f * rows + r, tiles, stride=late * slab), :]
                    value = jnp.where(mine, value, value + far)
                fields[k, f, r] = value
                values.append(value)
            for r in range(RIM[f]):
                top, bottom = values[r], values[rows - RIM[f] + r]
                first[k, FROM[f] + r] = jnp.where(odd, top, bottom)
                second[k, FROM[f] + r] = jnp.where(odd, bottom, top)


def step_kernel(low, order, fields, first, second, coef, *rest):
    whole, out, slots, sem, *held = rest[-7:]
    size, kinds, rows, tiles = fields.shape[:4]
    lane = lax.broadcasted_iota(jnp.int32, (tiles, LANES), 1)
    tile = lax.broadcasted_iota(jnp.int32, (tiles, LANES), 0)
    lane_first, lane_last = lane == 0, lane == LANES - 1
    wall_first = lane_first & (tile == 0)
    wall_last = lane_last & (tile == tiles - 1)
    half = 0.5 * DT
    odd = lax.axis_index("space") % 2 == 1
    known = pltpu.make_async_copy(order, slots, sem.at[size, 0])
    known.start()

    def difference(x, edge):
        before = pltpu.roll(jnp.where(lane_last, pltpu.roll(x, 1, 0), x), 1, 1)
        after = pltpu.roll(jnp.where(lane_first, pltpu.roll(x, tiles - 1, 0), x), LANES - 1, 1)
        return jnp.where(wall_last, edge, after) - jnp.where(wall_first, edge, before)

    def const(n, r):
        return coef[n, r + DEEP]

    def particle(k, carry):
        def get(n, f, r):
            if n:
                return held[f][n - 1, r + DEEP]
            if 0 <= r < rows:
                return fields[k, f, r]
            at = FROM[f] + (r + RIM[f] if r < 0 else r - rows)
            return jnp.where(odd == (r < 0), first[k, at], second[k, at])

        def put(n, f, r, value):
            if n < STEPS or f == 0:
                held[f][n - 1, r + DEEP] = value
            if n == STEPS and 0 <= r < rows:
                at = pl.ds(r // SUB * tiles * SUB + r % SUB, tiles, stride=SUB)
                out[k, f, at, :] = value

        for n in range(STEPS):
            left = STEPS - 1 - n
            low_u, high_u = (1 - 2 * left, rows + 2 * left - 1) if left else (0, rows)
            for r in range(-(2 * left + 1), rows + 2 * left + 1):
                across = difference(const(0, r) * get(n, 1, r), 0.0)
                along = const(0, r + 1) * get(n, 2, r + 1) - const(0, r - 1) * get(n, 2, r - 1)
                put(n + 1, 0, r, get(n, 0, r) - (across + along))
            if n + 1 == STEPS:
                pl.when(k == 0)(known.wait)
                copy_out(k, 0).start()
            for r in range(-2 * left, rows + 2 * left):
                uu, vv, c, s = get(n, 1, r), get(n, 2, r), const(1, r), const(2, r)
                if low_u <= r < high_u:
                    here = get(n + 1, 0, r)
                    put(n + 1, 1, r, s * (uu + c * vv - half * difference(here, here)))
                along = get(n + 1, 0, r + 1) - get(n + 1, 0, r - 1)
                put(n + 1, 2, r, s * (vv - c * uu - half * along))
                if n + 1 == STEPS and (r + 1) % SUB == 0:
                    copy_out(k, r // SUB + 1).start()
        return carry

    def copy_out(k, part):
        band = tiles * SUB
        at = (pl.ds(0, 1),) if part == 0 else (pl.ds(1, 2), pl.ds((part - 1) * band, band))
        return pltpu.make_async_copy(
            out.at[(k, *at)], whole.at[(slots[low + k], *at)], sem.at[k, part]
        )

    lax.fori_loop(0, size, particle, 0)
    for k in range(size):
        for part in range(rows // SUB + 1):
            copy_out(k, part).wait()


def local(ancestor, state, jitter, depth, coriolis, drag):
    members, kinds, rows, width = state.shape
    tiles, bands = width // LANES, rows // SUB
    blocks = lax.axis_size("dom")
    count = lax.axis_size("space")
    swap_first = [(i, i ^ 1) for i in range(count)]
    swap_second = [(i, (i + 2 * (i % 2) - 1) % count) for i in range(count)]
    f32 = jnp.float32

    def tiled(x):
        x = x.reshape(x.shape[:-2] + (x.shape[-2] // SUB, SUB, tiles, LANES))
        return jnp.swapaxes(x, -3, -2)

    state_t, jitter_t = tiled(state), tiled(jitter)

    packed = pl.pallas_call(
        functools.partial(pack_kernel, members),
        in_specs=[HB, HB],
        out_specs=HB,
        out_shape=jax.ShapeDtypeStruct((tiles, CAP, kinds, bands, SUB, LANES), f32),
        scratch_shapes=[
            pltpu.SMEM(ancestor.shape, jnp.int32),
            pltpu.VMEM((members, kinds, bands, tiles, SUB, LANES), f32),
            pltpu.SemaphoreType.DMA((2, CAP * kinds * bands)),
        ],
        compiler_params=PARAMS,
        name="pack",
    )(*(pltpu.with_memory_space_constraint(x, pltpu.HBM) for x in (ancestor, state_t)))
    table, order, gone, most = pl.pallas_call(
        functools.partial(plan_kernel, members),
        in_specs=[SM],
        out_specs=(SM, SM, SM, SM),
        out_shape=[
            jax.ShapeDtypeStruct((n,), jnp.int32) for n in (ancestor.shape[0], members, members, 1)
        ],
        scratch_shapes=[pltpu.SMEM((blocks,), jnp.int32)],
        compiler_params=PARAMS,
        name="plan",
    )(ancestor)

    sides = (members, kinds * rows * tiles, LANES)
    state_t, jitter_t = state_t.reshape(sides), jitter_t.reshape(sides)

    base = pl.pallas_call(
        base_kernel,
        in_specs=[SM, SM, VM, VM],
        out_specs=VM,
        out_shape=jax.ShapeDtypeStruct((members, kinds, rows, tiles, LANES), f32),
        compiler_params=PARAMS,
        name="base",
    )(order, gone, state_t, jitter_t)

    packed, *raw = lax.optimization_barrier((packed, depth, coriolis, drag))
    pieces = lax.all_to_all(packed, "dom", 0, 0, tiled=True)
    pieces = pieces.reshape(blocks * CAP, kinds * rows, LANES)
    rim = jax.ShapeDtypeStruct((3, tiles // 2, SUB, LANES), f32)
    rims = pl.pallas_call(
        rim_kernel,
        in_specs=[HB] * 3,
        out_specs=(VM, VM),
        out_shape=(rim, rim),
        scratch_shapes=[pltpu.SemaphoreType.DMA((6,))],
        compiler_params=PARAMS,
        name="rims",
    )(*(pltpu.with_memory_space_constraint(tiled(x), pltpu.HBM) for x in raw))
    rims = [lax.ppermute(rims[0], "space", swap_first), lax.ppermute(rims[1], "space", swap_second)]
    *rims, table, order, gone, base = lax.optimization_barrier((*rims, table, order, gone, base))
    rims += [lax.ppermute(x, "dom", [(i, i ^ 1) for i in range(blocks)]) for x in rims]
    coef = pl.pallas_call(
        coef_kernel,
        in_specs=[VM] * 7,
        out_specs=VM,
        out_shape=jax.ShapeDtypeStruct((3, rows + 2 * DEEP, tiles, LANES), f32),
        compiler_params=PARAMS,
        name="coef",
    )(
        *(tiled(x).reshape(rows * tiles, LANES) for x in raw),
        *(x.reshape(-1, LANES) for x in rims),
    )
    def prepared(low, size, gone, base, routed):
        rim = jax.ShapeDtypeStruct((size, RIMS, tiles, LANES), f32)
        fields, first, second = pl.pallas_call(
            functools.partial(prep_kernel, low),
            in_specs=[SM, VM, VM],
            out_specs=(VM, VM, VM),
            out_shape=(jax.ShapeDtypeStruct((size, kinds, rows, tiles, LANES), f32), rim, rim),
            compiler_params=PARAMS,
            name="prep",
        )(gone, base, routed)
        first = lax.ppermute(first, "space", swap_first)
        second = lax.ppermute(second, "space", swap_second)
        return fields, first, second

    def stepped(low, size, order, parts, coef, out):
        return pl.pallas_call(
            functools.partial(step_kernel, low),
            in_specs=[HB] + [VM] * 4 + [HB] * len(out),
            out_specs=HB,
            out_shape=jax.ShapeDtypeStruct((members, kinds, rows * tiles, LANES), f32),
            scratch_shapes=[
                pltpu.VMEM((size, kinds, rows * tiles, LANES), f32),
                pltpu.SMEM((members,), jnp.int32),
                pltpu.SemaphoreType.DMA((size + 1, bands + 1)),
            ]
            + [pltpu.VMEM((STEPS, rows + 2 * DEEP, tiles, LANES), f32)] * 3,
            input_output_aliases={5: 0} if out else {},
            compiler_params=PARAMS,
            name="steps",
        )(order, *parts, coef, *out)

    def rest(late, pieces, coef, table, order, gone, base):
        chosen = pl.pallas_call(
            functools.partial(pick_kernel, members),
            in_specs=[SM, VM],
            out_specs=VM,
            out_shape=jax.ShapeDtypeStruct((blocks, late, kinds * rows, LANES), f32),
            compiler_params=PARAMS,
            name="pick",
        )(table, pieces)
        routed = lax.all_to_all(chosen, "dom", 0, 0, tiled=True).reshape(-1, LANES)
        routed, base = lax.optimization_barrier((routed, base))
        low = 0
        chunks = []
        for size in CHUNKS:
            chunks.append((low, size, prepared(low, size, gone, base, routed)))
            low += size
        out = []
        for low, size, parts in chunks:
            out = [stepped(low, size, order, parts, coef, out)]
        return out[0]

    args = lax.optimization_barrier((pieces, coef, table, order, gone, base))
    which = jnp.clip(most[0] - SIZES[0], 0, len(SIZES) - 1)
    out = lax.switch(which, [functools.partial(rest, size) for size in SIZES], *args)
    out = out.reshape(members, kinds, bands, tiles, SUB, LANES)
    return jnp.swapaxes(out, -3, -2).reshape(state.shape)


def solution(mesh):
    placed = (
        P(),
        P("dom", None, "space", None),
        P("dom", None, "space", None),
        P("space", None),
        P("space", None),
        P("space", None),
    )
    return jax.shard_map(
        local, mesh=mesh, in_specs=placed, out_specs=P("dom", None, "space", None), check_vma=False
    )
```

```python
import functools

import jax
import jax.numpy as jnp
from jax import lax
from jax.experimental import pallas as pl
from jax.experimental.pallas import tpu as pltpu
from jax.sharding import PartitionSpec as P

STEPS = 4
CAP = 2
DT = 0.3
LANES = 128
SUB = 8
DEEP = 8
RIM = (7, 7, 8)
RIMS = sum(RIM)
FROM = (0, 7, 14)
CHUNKS = (2, 2)
SIZES = (2, 3, 4)

VM = pl.BlockSpec(memory_space=pltpu.VMEM)
SM = pl.BlockSpec(memory_space=pltpu.SMEM)
HB = pl.BlockSpec(memory_space=pltpu.HBM)
PARAMS = pltpu.CompilerParams(vmem_limit_bytes=24 << 20)


def pack_kernel(members, ancestor, depth, coriolis, drag, state, out, near, far, anc, held, sem):
    shift = members.bit_length() - 1
    known = pltpu.make_async_copy(ancestor, anc, sem.at[0, members])
    known.start()
    fetched = [pltpu.make_async_copy(state.at[k], held.at[k], sem.at[0, k]) for k in range(members)]
    for c in fetched:
        c.start()
    toward = 1 - lax.axis_index("space") % 2
    last = depth.shape[0] - 1
    part = near.shape[1]
    mine = pl.ds(lax.axis_index("dom") % 2 * part, part)
    rims = []
    for n, ref in enumerate((depth, coriolis, drag)):
        for rim, at in ((near, toward * last), (far, (1 - toward) * last)):
            used = sem.at[0, members + 1 + len(rims)]
            rims.append(pltpu.make_async_copy(ref.at[at, mine], rim.at[n], used))
    for c in rims:
        c.start()
    known.wait()
    me = lax.axis_index("dom")
    bits = jnp.int32(0)
    for j in range(anc.shape[0]):
        a = anc[j]
        hit = (a != j) & ((a >> shift) == me)
        bits = bits | jnp.where(hit, jnp.left_shift(1, (a & (members - 1))), 0)
    first = jnp.int32(members - 1)
    for k in reversed(range(members)):
        first = jnp.where((bits >> k) & 1 == 1, k, first)
    second = jnp.int32(members - 1)
    for k in reversed(range(members)):
        second = jnp.where(((bits >> k) & 1 == 1) & (k != first), k, second)
    for c in fetched:
        c.wait()
    copies = []
    for q, p in enumerate((first, second)):
        for f in range(state.shape[1]):
            for t in range(state.shape[2]):
                copies.append(
                    pltpu.make_async_copy(held.at[p, f, t], out.at[:, q, f, t], sem.at[1, len(copies)])
                )
    for c in copies:
        c.start()
    for c in rims + copies:
        c.wait()


def plan_kernel(members, anc, table, order, gone, most, donors):
    slots = anc.shape[0]
    shift = members.bit_length() - 1
    for b in range(slots // members):
        donors[b] = 0
    for j in range(slots):
        a = anc[j]
        donors[(a >> shift)] |= jnp.where(a != j, jnp.left_shift(1, (a & (members - 1))), 0)
    worst = jnp.int32(0)
    for b in range(slots // members):
        moved = [jnp.where(anc[b * members + k] != b * members + k, 1, 0) for k in range(members)]
        stay = members - sum(moved)
        worst = jnp.maximum(worst, members - stay)
        ahead = jnp.int32(0)
        for k in range(members):
            a = anc[b * members + k]
            below = donors[(a >> shift)] & (jnp.left_shift(1, (a & (members - 1))) - 1)
            turn = jnp.where(moved[k] == 1, stay + ahead, k - ahead)
            table[b * members + turn] = (a >> shift) * CAP + jnp.where(below != 0, 1, 0)
            ahead += moved[k]
    most[0] = worst
    at = lax.axis_index("dom") * members
    moved = [jnp.where(anc[at + k] != at + k, 1, 0) for k in range(members)]
    stay = members - sum(moved)
    ahead = jnp.int32(0)
    for k in range(members):
        turn = jnp.where(moved[k] == 1, stay + ahead, k - ahead)
        order[turn] = k
        gone[turn] = moved[k]
        ahead += moved[k]


def coef_kernel(depth, coriolis, drag, first, second, first_other, second_other, out):
    tiles = out.shape[2]
    part = tiles // 2
    bands = depth.shape[0] // (tiles * SUB)
    odd = lax.axis_index("space") % 2 == 1
    high = lax.axis_index("dom") % 2 == 1
    for r in range(out.shape[1]):
        band, row = r // SUB - 1, r % SUB
        values = []
        for n, own in enumerate((depth, coriolis, drag)):
            if 0 <= band < bands:
                values.append(own[pl.ds(band * tiles * SUB + row, tiles, stride=SUB), :])
            else:
                at = pl.ds(n * part * SUB + row, part, stride=SUB)
                ahead = odd == (band < 0)
                mine = jnp.where(ahead, first[at, :], second[at, :])
                other = jnp.where(ahead, first_other[at, :], second_other[at, :])
                halves = jnp.where(high, other, mine), jnp.where(high, mine, other)
                values.append(jnp.concatenate(halves, axis=0))
        out[0, r] = (0.5 * DT) * values[0]
        out[1, r] = DT * values[1]
        out[2, r] = 1.0 / (1.0 + DT * values[2])


def pick_kernel(members, table, got, out):
    size = out.shape[1]
    for d in range(out.shape[0]):
        for k in range(size):
            out[d, k] = got[table[(d + 1) * members - size + k]]


def base_kernel(order, gone, state, jitter, out):
    members, kinds, rows, tiles = out.shape[:4]
    for k in range(members):
        slot = order[k]
        mine = gone[k] == 0
        for f in range(kinds):
            for r in range(rows):
                near = pl.ds((f * (rows // SUB) + r // SUB) * tiles * SUB + r % SUB, tiles, stride=SUB)
                out[k, f, r] = jnp.where(mine, state[slot, near, :], 0.0) + jitter[slot, near, :]


def prep_kernel(low, gone, base, routed, fields, first, second):
    size, kinds, rows, tiles = fields.shape[:4]
    slab = kinds * rows
    late = routed.shape[0] // (tiles * slab)
    odd = lax.axis_index("space") % 2 == 1
    for k in range(size):
        at = low + k - (base.shape[0] - late)
        mine = gone[low + k] == 0
        for f in range(kinds):
            values = []
            for r in range(rows):
                value = base[low + k, f, r]
                if at >= 0:
                    far = routed[pl.ds(at * slab + f * rows + r, tiles, stride=late * slab), :]
                    value = jnp.where(mine, value, value + far)
                fields[k, f, r] = value
                values.append(value)
            for r in range(RIM[f]):
                top, bottom = values[r], values[rows - RIM[f] + r]
                first[k, FROM[f] + r] = jnp.where(odd, top, bottom)
                second[k, FROM[f] + r] = jnp.where(odd, bottom, top)


def step_kernel(low, order, fields, first, second, coef, *rest):
    whole, out, slots, sem, *held = rest[-7:]
    size, kinds, rows, tiles = fields.shape[:4]
    lane = lax.broadcasted_iota(jnp.int32, (tiles, LANES), 1)
    tile = lax.broadcasted_iota(jnp.int32, (tiles, LANES), 0)
    lane_first, lane_last = lane == 0, lane == LANES - 1
    wall_first = lane_first & (tile == 0)
    wall_last = lane_last & (tile == tiles - 1)
    half = 0.5 * DT
    odd = lax.axis_index("space") % 2 == 1
    known = pltpu.make_async_copy(order, slots, sem.at[size, 0])
    known.start()

    def difference(x, edge):
        before = pltpu.roll(jnp.where(lane_last, pltpu.roll(x, 1, 0), x), 1, 1)
        after = pltpu.roll(jnp.where(lane_first, pltpu.roll(x, tiles - 1, 0), x), LANES - 1, 1)
        return jnp.where(wall_last, edge, after) - jnp.where(wall_first, edge, before)

    def const(n, r):
        return coef[n, r + DEEP]

    def particle(k, carry):
        def get(n, f, r):
            if n:
                return held[f][n - 1, r + DEEP]
            if 0 <= r < rows:
                return fields[k, f, r]
            at = FROM[f] + (r + RIM[f] if r < 0 else r - rows)
            return jnp.where(odd == (r < 0), first[k, at], second[k, at])

        def put(n, f, r, value):
            if n < STEPS or f == 0:
                held[f][n - 1, r + DEEP] = value
            if n == STEPS and 0 <= r < rows:
                at = pl.ds(r // SUB * tiles * SUB + r % SUB, tiles, stride=SUB)
                out[k, f, at, :] = value

        for n in range(STEPS):
            left = STEPS - 1 - n
            low_u, high_u = (1 - 2 * left, rows + 2 * left - 1) if left else (0, rows)
            for r in range(-(2 * left + 1), rows + 2 * left + 1):
                across = difference(const(0, r) * get(n, 1, r), 0.0)
                along = const(0, r + 1) * get(n, 2, r + 1) - const(0, r - 1) * get(n, 2, r - 1)
                put(n + 1, 0, r, get(n, 0, r) - (across + along))
            if n + 1 == STEPS:
                pl.when(k == 0)(known.wait)
                copy_out(k, 0).start()
            for r in range(-2 * left, rows + 2 * left):
                uu, vv, c, s = get(n, 1, r), get(n, 2, r), const(1, r), const(2, r)
                if low_u <= r < high_u:
                    here = get(n + 1, 0, r)
                    put(n + 1, 1, r, s * (uu + c * vv - half * difference(here, here)))
                along = get(n + 1, 0, r + 1) - get(n + 1, 0, r - 1)
                put(n + 1, 2, r, s * (vv - c * uu - half * along))
                if n + 1 == STEPS and (r + 1) % SUB == 0:
                    copy_out(k, r // SUB + 1).start()
        return carry

    def copy_out(k, part):
        band = tiles * SUB
        at = (pl.ds(0, 1),) if part == 0 else (pl.ds(1, 2), pl.ds((part - 1) * band, band))
        return pltpu.make_async_copy(
            out.at[(k, *at)], whole.at[(slots[low + k], *at)], sem.at[k, part]
        )

    lax.fori_loop(0, size, particle, 0)
    for k in range(size):
        for part in range(rows // SUB + 1):
            copy_out(k, part).wait()


def local(ancestor, state, jitter, depth, coriolis, drag):
    members, kinds, rows, width = state.shape
    tiles, bands = width // LANES, rows // SUB
    blocks = lax.axis_size("dom")
    count = lax.axis_size("space")
    swap_first = [(i, i ^ 1) for i in range(count)]
    swap_second = [(i, (i + 2 * (i % 2) - 1) % count) for i in range(count)]
    f32 = jnp.float32

    def tiled(x):
        x = x.reshape(x.shape[:-2] + (x.shape[-2] // SUB, SUB, tiles, LANES))
        return jnp.swapaxes(x, -3, -2)

    state_t, jitter_t = tiled(state), tiled(jitter)

    raw = (depth, coriolis, drag)
    rim = jax.ShapeDtypeStruct((3, tiles // 2, SUB, LANES), f32)
    packed, *rims = pl.pallas_call(
        functools.partial(pack_kernel, members),
        in_specs=[HB] * 5,
        out_specs=(HB, VM, VM),
        out_shape=(pltpu.HBM((tiles, CAP, kinds, bands, SUB, LANES), f32), rim, rim),
        scratch_shapes=[
            pltpu.SMEM(ancestor.shape, jnp.int32),
            pltpu.VMEM((members, kinds, bands, tiles, SUB, LANES), f32),
            pltpu.SemaphoreType.DMA((2, CAP * kinds * bands)),
        ],
        compiler_params=PARAMS,
        name="pack",
    )(
        *(
            pltpu.with_memory_space_constraint(x, pltpu.HBM)
            for x in (ancestor, *(tiled(x) for x in raw), state_t)
        )
    )
    pieces = lax.all_to_all(packed, "dom", 0, 0, tiled=True)
    pieces = pieces.reshape(blocks * CAP, kinds * rows, LANES)

    table, order, gone, most = pl.pallas_call(
        functools.partial(plan_kernel, members),
        in_specs=[SM],
        out_specs=(SM, SM, SM, SM),
        out_shape=[
            jax.ShapeDtypeStruct((n,), jnp.int32) for n in (ancestor.shape[0], members, members, 1)
        ],
        scratch_shapes=[pltpu.SMEM((blocks,), jnp.int32)],
        compiler_params=PARAMS,
        name="plan",
    )(ancestor)

    sides = (members, kinds * rows * tiles, LANES)
    state_t, jitter_t = state_t.reshape(sides), jitter_t.reshape(sides)

    base = pl.pallas_call(
        base_kernel,
        in_specs=[SM, SM, VM, VM],
        out_specs=VM,
        out_shape=jax.ShapeDtypeStruct((members, kinds, rows, tiles, LANES), f32),
        compiler_params=PARAMS,
        name="base",
    )(order, gone, state_t, jitter_t)

    rims = [lax.ppermute(rims[0], "space", swap_first), lax.ppermute(rims[1], "space", swap_second)]
    *rims, table, order, gone, base = lax.optimization_barrier((*rims, table, order, gone, base))
    rims += [lax.ppermute(x, "dom", [(i, i ^ 1) for i in range(blocks)]) for x in rims]
    coef = pl.pallas_call(
        coef_kernel,
        in_specs=[VM] * 7,
        out_specs=VM,
        out_shape=jax.ShapeDtypeStruct((3, rows + 2 * DEEP, tiles, LANES), f32),
        compiler_params=PARAMS,
        name="coef",
    )(
        *(tiled(x).reshape(rows * tiles, LANES) for x in raw),
        *(x.reshape(-1, LANES) for x in rims),
    )
    def prepared(low, size, gone, base, routed):
        rim = jax.ShapeDtypeStruct((size, RIMS, tiles, LANES), f32)
        fields, first, second = pl.pallas_call(
            functools.partial(prep_kernel, low),
            in_specs=[SM, VM, VM],
            out_specs=(VM, VM, VM),
            out_shape=(jax.ShapeDtypeStruct((size, kinds, rows, tiles, LANES), f32), rim, rim),
            compiler_params=PARAMS,
            name="prep",
        )(gone, base, routed)
        first = lax.ppermute(first, "space", swap_first)
        second = lax.ppermute(second, "space", swap_second)
        return fields, first, second

    def stepped(low, size, order, parts, coef, out):
        return pl.pallas_call(
            functools.partial(step_kernel, low),
            in_specs=[HB] + [VM] * 4 + [HB] * len(out),
            out_specs=HB,
            out_shape=jax.ShapeDtypeStruct((members, kinds, rows * tiles, LANES), f32),
            scratch_shapes=[
                pltpu.VMEM((size, kinds, rows * tiles, LANES), f32),
                pltpu.SMEM((members,), jnp.int32),
                pltpu.SemaphoreType.DMA((size + 1, bands + 1)),
            ]
            + [pltpu.VMEM((STEPS, rows + 2 * DEEP, tiles, LANES), f32)] * 3,
            input_output_aliases={5: 0} if out else {},
            compiler_params=PARAMS,
            name="steps",
        )(order, *parts, coef, *out)

    def rest(late, pieces, coef, table, order, gone, base):
        chosen = pl.pallas_call(
            functools.partial(pick_kernel, members),
            in_specs=[SM, VM],
            out_specs=VM,
            out_shape=jax.ShapeDtypeStruct((blocks, late, kinds * rows, LANES), f32),
            compiler_params=PARAMS,
            name="pick",
        )(table, pieces)
        routed = lax.all_to_all(chosen, "dom", 0, 0, tiled=True).reshape(-1, LANES)
        routed, base = lax.optimization_barrier((routed, base))
        low = 0
        chunks = []
        for size in CHUNKS:
            chunks.append((low, size, prepared(low, size, gone, base, routed)))
            low += size
        out = []
        for low, size, parts in chunks:
            out = [stepped(low, size, order, parts, coef, out)]
        return out[0]

    args = lax.optimization_barrier((pieces, coef, table, order, gone, base))
    which = jnp.clip(most[0] - SIZES[0], 0, len(SIZES) - 1)
    out = lax.switch(which, [functools.partial(rest, size) for size in SIZES], *args)
    out = out.reshape(members, kinds, bands, tiles, SUB, LANES)
    return jnp.swapaxes(out, -3, -2).reshape(state.shape)


def solution(mesh):
    placed = (
        P(),
        P("dom", None, "space", None),
        P("dom", None, "space", None),
        P("space", None),
        P("space", None),
        P("space", None),
    )
    return jax.shard_map(
        local, mesh=mesh, in_specs=placed, out_specs=P("dom", None, "space", None), check_vma=False
    )
```

```python
import functools

import jax
import jax.numpy as jnp
from jax import lax
from jax.experimental import pallas as pl
from jax.experimental.pallas import tpu as pltpu
from jax.sharding import PartitionSpec as P

STEPS = 4
CAP = 2
DT = 0.3
LANES = 128
SUB = 8
DEEP = 8
RIM = (7, 7, 8)
RIMS = sum(RIM)
FROM = (0, 7, 14)
CHUNKS = (2, 2)
SIZES = (2, 3, 4)

VM = pl.BlockSpec(memory_space=pltpu.VMEM)
SM = pl.BlockSpec(memory_space=pltpu.SMEM)
HB = pl.BlockSpec(memory_space=pltpu.HBM)
PARAMS = pltpu.CompilerParams(vmem_limit_bytes=24 << 20)


def pack_kernel(members, ancestor, depth, coriolis, drag, state, out, near, far, anc, held, sem):
    shift = members.bit_length() - 1
    known = pltpu.make_async_copy(ancestor, anc, sem.at[0, members])
    known.start()
    fetched = [pltpu.make_async_copy(state.at[k], held.at[k], sem.at[0, k]) for k in range(members)]
    for c in fetched:
        c.start()
    toward = lax.axis_index("space") % 2
    last = depth.shape[0] - 1
    part = near.shape[1]
    mine = pl.ds(lax.axis_index("dom") % 2 * part, part)
    rims = []
    for n, ref in enumerate((depth, coriolis, drag)):
        for rim, at in ((near, toward * last), (far, (1 - toward) * last)):
            used = sem.at[0, members + 1 + len(rims)]
            rims.append(pltpu.make_async_copy(ref.at[at, mine], rim.at[n], used))
    for c in rims:
        c.start()
    known.wait()
    me = lax.axis_index("dom")
    bits = jnp.int32(0)
    for j in range(anc.shape[0]):
        a = anc[j]
        hit = (a != j) & ((a >> shift) == me)
        bits = bits | jnp.where(hit, jnp.left_shift(1, (a & (members - 1))), 0)
    first = jnp.int32(members - 1)
    for k in reversed(range(members)):
        first = jnp.where((bits >> k) & 1 == 1, k, first)
    second = jnp.int32(members - 1)
    for k in reversed(range(members)):
        second = jnp.where(((bits >> k) & 1 == 1) & (k != first), k, second)
    for c in fetched:
        c.wait()
    copies = []
    for q, p in enumerate((first, second)):
        for f in range(state.shape[1]):
            for t in range(state.shape[2]):
                copies.append(
                    pltpu.make_async_copy(held.at[p, f, t], out.at[:, q, f, t], sem.at[1, len(copies)])
                )
    for c in copies:
        c.start()
    for c in rims + copies:
        c.wait()


def plan_kernel(members, anc, table, order, gone, most, donors):
    slots = anc.shape[0]
    shift = members.bit_length() - 1
    for b in range(slots // members):
        donors[b] = 0
    for j in range(slots):
        a = anc[j]
        donors[(a >> shift)] |= jnp.where(a != j, jnp.left_shift(1, (a & (members - 1))), 0)
    worst = jnp.int32(0)
    for b in range(slots // members):
        moved = [jnp.where(anc[b * members + k] != b * members + k, 1, 0) for k in range(members)]
        stay = members - sum(moved)
        worst = jnp.maximum(worst, members - stay)
        ahead = jnp.int32(0)
        for k in range(members):
            a = anc[b * members + k]
            below = donors[(a >> shift)] & (jnp.left_shift(1, (a & (members - 1))) - 1)
            turn = jnp.where(moved[k] == 1, stay + ahead, k - ahead)
            table[b * members + turn] = (a >> shift) * CAP + jnp.where(below != 0, 1, 0)
            ahead += moved[k]
    most[0] = worst
    at = lax.axis_index("dom") * members
    moved = [jnp.where(anc[at + k] != at + k, 1, 0) for k in range(members)]
    stay = members - sum(moved)
    ahead = jnp.int32(0)
    for k in range(members):
        turn = jnp.where(moved[k] == 1, stay + ahead, k - ahead)
        order[turn] = k
        gone[turn] = moved[k]
        ahead += moved[k]


def coef_kernel(depth, coriolis, drag, first, second, first_other, second_other, out):
    tiles = out.shape[2]
    part = tiles // 2
    bands = depth.shape[0] // (tiles * SUB)
    even = lax.axis_index("space") % 2 == 0
    high = lax.axis_index("dom") % 2 == 1
    for r in range(out.shape[1]):
        band, row = r // SUB - 1, r % SUB
        values = []
        for n, own in enumerate((depth, coriolis, drag)):
            if 0 <= band < bands:
                values.append(own[pl.ds(band * tiles * SUB + row, tiles, stride=SUB), :])
            else:
                at = pl.ds(n * part * SUB + row, part, stride=SUB)
                ahead = even == (band < 0)
                mine = jnp.where(ahead, first[at, :], second[at, :])
                other = jnp.where(ahead, first_other[at, :], second_other[at, :])
                halves = jnp.where(high, other, mine), jnp.where(high, mine, other)
                values.append(jnp.concatenate(halves, axis=0))
        out[0, r] = (0.5 * DT) * values[0]
        out[1, r] = DT * values[1]
        out[2, r] = 1.0 / (1.0 + DT * values[2])


def pick_kernel(members, table, got, out):
    size = out.shape[1]
    for d in range(out.shape[0]):
        for k in range(size):
            out[d, k] = got[table[(d + 1) * members - size + k]]


def base_kernel(order, gone, state, jitter, out):
    members, kinds, rows, tiles = out.shape[:4]
    for k in range(members):
        slot = order[k]
        mine = gone[k] == 0
        for f in range(kinds):
            for r in range(rows):
                near = pl.ds((f * (rows // SUB) + r // SUB) * tiles * SUB + r % SUB, tiles, stride=SUB)
                out[k, f, r] = jnp.where(mine, state[slot, near, :], 0.0) + jitter[slot, near, :]


def prep_kernel(low, gone, base, routed, fields, first, second):
    size, kinds, rows, tiles = fields.shape[:4]
    slab = kinds * rows
    late = routed.shape[0] // (tiles * slab)
    even = lax.axis_index("space") % 2 == 0
    for k in range(size):
        at = low + k - (base.shape[0] - late)
        mine = gone[low + k] == 0
        for f in range(kinds):
            values = []
            for r in range(rows):
                value = base[low + k, f, r]
                if at >= 0:
                    far = routed[pl.ds(at * slab + f * rows + r, tiles, stride=late * slab), :]
                    value = jnp.where(mine, value, value + far)
                fields[k, f, r] = value
                values.append(value)
            for r in range(RIM[f]):
                top, bottom = values[r], values[rows - RIM[f] + r]
                first[k, FROM[f] + r] = jnp.where(even, top, bottom)
                second[k, FROM[f] + r] = jnp.where(even, bottom, top)


def step_kernel(low, order, fields, first, second, coef, *rest):
    whole, out, slots, sem, *held = rest[-7:]
    size, kinds, rows, tiles = fields.shape[:4]
    lane = lax.broadcasted_iota(jnp.int32, (tiles, LANES), 1)
    tile = lax.broadcasted_iota(jnp.int32, (tiles, LANES), 0)
    lane_first, lane_last = lane == 0, lane == LANES - 1
    wall_first = lane_first & (tile == 0)
    wall_last = lane_last & (tile == tiles - 1)
    half = 0.5 * DT
    even = lax.axis_index("space") % 2 == 0
    known = pltpu.make_async_copy(order, slots, sem.at[size, 0])
    known.start()

    def difference(x, edge):
        before = pltpu.roll(jnp.where(lane_last, pltpu.roll(x, 1, 0), x), 1, 1)
        after = pltpu.roll(jnp.where(lane_first, pltpu.roll(x, tiles - 1, 0), x), LANES - 1, 1)
        return jnp.where(wall_last, edge, after) - jnp.where(wall_first, edge, before)

    def const(n, r):
        return coef[n, r + DEEP]

    def particle(k, carry):
        def get(n, f, r):
            if n:
                return held[f][n - 1, r + DEEP]
            if 0 <= r < rows:
                return fields[k, f, r]
            at = FROM[f] + (r + RIM[f] if r < 0 else r - rows)
            return jnp.where(even == (r < 0), first[k, at], second[k, at])

        def put(n, f, r, value):
            if n < STEPS or f == 0:
                held[f][n - 1, r + DEEP] = value
            if n == STEPS and 0 <= r < rows:
                at = pl.ds(r // SUB * tiles * SUB + r % SUB, tiles, stride=SUB)
                out[k, f, at, :] = value

        for n in range(STEPS):
            left = STEPS - 1 - n
            low_u, high_u = (1 - 2 * left, rows + 2 * left - 1) if left else (0, rows)
            for r in range(-(2 * left + 1), rows + 2 * left + 1):
                across = difference(const(0, r) * get(n, 1, r), 0.0)
                along = const(0, r + 1) * get(n, 2, r + 1) - const(0, r - 1) * get(n, 2, r - 1)
                put(n + 1, 0, r, get(n, 0, r) - (across + along))
            if n + 1 == STEPS:
                pl.when(k == 0)(known.wait)
                copy_out(k, 0).start()
            for r in range(-2 * left, rows + 2 * left):
                uu, vv, c, s = get(n, 1, r), get(n, 2, r), const(1, r), const(2, r)
                if low_u <= r < high_u:
                    here = get(n + 1, 0, r)
                    put(n + 1, 1, r, s * (uu + c * vv - half * difference(here, here)))
                along = get(n + 1, 0, r + 1) - get(n + 1, 0, r - 1)
                put(n + 1, 2, r, s * (vv - c * uu - half * along))
                if n + 1 == STEPS and (r + 1) % SUB == 0:
                    copy_out(k, r // SUB + 1).start()
        return carry

    def copy_out(k, part):
        band = tiles * SUB
        at = (pl.ds(0, 1),) if part == 0 else (pl.ds(1, 2), pl.ds((part - 1) * band, band))
        return pltpu.make_async_copy(
            out.at[(k, *at)], whole.at[(slots[low + k], *at)], sem.at[k, part]
        )

    lax.fori_loop(0, size, particle, 0)
    for k in range(size):
        for part in range(rows // SUB + 1):
            copy_out(k, part).wait()


def local(ancestor, state, jitter, depth, coriolis, drag):
    members, kinds, rows, width = state.shape
    tiles, bands = width // LANES, rows // SUB
    blocks = lax.axis_size("dom")
    count = lax.axis_size("space")
    swap_first = [(i, (i + 2 * (i % 2) - 1) % count) for i in range(count)]
    swap_second = [(i, i ^ 1) for i in range(count)]
    f32 = jnp.float32

    def tiled(x):
        x = x.reshape(x.shape[:-2] + (x.shape[-2] // SUB, SUB, tiles, LANES))
        return jnp.swapaxes(x, -3, -2)

    state_t, jitter_t = tiled(state), tiled(jitter)

    raw = (depth, coriolis, drag)
    rim = jax.ShapeDtypeStruct((3, tiles // 2, SUB, LANES), f32)
    packed, *rims = pl.pallas_call(
        functools.partial(pack_kernel, members),
        in_specs=[HB] * 5,
        out_specs=(HB, VM, VM),
        out_shape=(pltpu.HBM((tiles, CAP, kinds, bands, SUB, LANES), f32), rim, rim),
        scratch_shapes=[
            pltpu.SMEM(ancestor.shape, jnp.int32),
            pltpu.VMEM((members, kinds, bands, tiles, SUB, LANES), f32),
            pltpu.SemaphoreType.DMA((2, CAP * kinds * bands)),
        ],
        compiler_params=PARAMS,
        name="pack",
    )(
        *(
            pltpu.with_memory_space_constraint(x, pltpu.HBM)
            for x in (ancestor, *(tiled(x) for x in raw), state_t)
        )
    )
    pieces = lax.all_to_all(packed, "dom", 0, 0, tiled=True)
    pieces = pieces.reshape(blocks * CAP, kinds * rows, LANES)

    table, order, gone, most = pl.pallas_call(
        functools.partial(plan_kernel, members),
        in_specs=[SM],
        out_specs=(SM, SM, SM, SM),
        out_shape=[
            jax.ShapeDtypeStruct((n,), jnp.int32) for n in (ancestor.shape[0], members, members, 1)
        ],
        scratch_shapes=[pltpu.SMEM((blocks,), jnp.int32)],
        compiler_params=PARAMS,
        name="plan",
    )(ancestor)

    sides = (members, kinds * rows * tiles, LANES)
    state_t, jitter_t = state_t.reshape(sides), jitter_t.reshape(sides)

    base = pl.pallas_call(
        base_kernel,
        in_specs=[SM, SM, VM, VM],
        out_specs=VM,
        out_shape=jax.ShapeDtypeStruct((members, kinds, rows, tiles, LANES), f32),
        compiler_params=PARAMS,
        name="base",
    )(order, gone, state_t, jitter_t)

    rims = [lax.ppermute(rims[0], "space", swap_first), lax.ppermute(rims[1], "space", swap_second)]
    *rims, table, order, gone, base = lax.optimization_barrier((*rims, table, order, gone, base))
    rims += [lax.ppermute(x, "dom", [(i, i ^ 1) for i in range(blocks)]) for x in rims]
    coef = pl.pallas_call(
        coef_kernel,
        in_specs=[VM] * 7,
        out_specs=VM,
        out_shape=jax.ShapeDtypeStruct((3, rows + 2 * DEEP, tiles, LANES), f32),
        compiler_params=PARAMS,
        name="coef",
    )(
        *(tiled(x).reshape(rows * tiles, LANES) for x in raw),
        *(x.reshape(-1, LANES) for x in rims),
    )
    def prepared(low, size, gone, base, routed):
        rim = jax.ShapeDtypeStruct((size, RIMS, tiles, LANES), f32)
        fields, first, second = pl.pallas_call(
            functools.partial(prep_kernel, low),
            in_specs=[SM, VM, VM],
            out_specs=(VM, VM, VM),
            out_shape=(jax.ShapeDtypeStruct((size, kinds, rows, tiles, LANES), f32), rim, rim),
            compiler_params=PARAMS,
            name="prep",
        )(gone, base, routed)
        first = lax.ppermute(first, "space", swap_first)
        second = lax.ppermute(second, "space", swap_second)
        return fields, first, second

    def stepped(low, size, order, parts, coef, out):
        return pl.pallas_call(
            functools.partial(step_kernel, low),
            in_specs=[HB] + [VM] * 4 + [HB] * len(out),
            out_specs=HB,
            out_shape=jax.ShapeDtypeStruct((members, kinds, rows * tiles, LANES), f32),
            scratch_shapes=[
                pltpu.VMEM((size, kinds, rows * tiles, LANES), f32),
                pltpu.SMEM((members,), jnp.int32),
                pltpu.SemaphoreType.DMA((size + 1, bands + 1)),
            ]
            + [pltpu.VMEM((STEPS, rows + 2 * DEEP, tiles, LANES), f32)] * 3,
            input_output_aliases={5: 0} if out else {},
            compiler_params=PARAMS,
            name="steps",
        )(order, *parts, coef, *out)

    def rest(late, pieces, coef, table, order, gone, base):
        chosen = pl.pallas_call(
            functools.partial(pick_kernel, members),
            in_specs=[SM, VM],
            out_specs=VM,
            out_shape=jax.ShapeDtypeStruct((blocks, late, kinds * rows, LANES), f32),
            compiler_params=PARAMS,
            name="pick",
        )(table, pieces)
        routed = lax.all_to_all(chosen, "dom", 0, 0, tiled=True).reshape(-1, LANES)
        routed, base = lax.optimization_barrier((routed, base))
        low = 0
        chunks = []
        for size in CHUNKS:
            chunks.append((low, size, prepared(low, size, gone, base, routed)))
            low += size
        out = []
        for low, size, parts in chunks:
            out = [stepped(low, size, order, parts, coef, out)]
        return out[0]

    args = lax.optimization_barrier((pieces, coef, table, order, gone, base))
    which = jnp.clip(most[0] - SIZES[0], 0, len(SIZES) - 1)
    out = lax.switch(which, [functools.partial(rest, size) for size in SIZES], *args)
    out = out.reshape(members, kinds, bands, tiles, SUB, LANES)
    return jnp.swapaxes(out, -3, -2).reshape(state.shape)


def solution(mesh):
    placed = (
        P(),
        P("dom", None, "space", None),
        P("dom", None, "space", None),
        P("space", None),
        P("space", None),
        P("space", None),
    )
    return jax.shard_map(
        local, mesh=mesh, in_specs=placed, out_specs=P("dom", None, "space", None), check_vma=False
    )
```
